32 devices in a mesh: groups: 2 (over y), seq: 16 (over z, x, core).
Axes of the slice: x: 2, y: 2, z: 4, core: 2. Of those that a mesh axis runs over, the one named last changes fastest.
Arguments:
- token_ids: int32 [4096], P('groups'), parts along dimension 0, may hold values from 0 to 511
- vocab_table: bfloat16 [512, 3, 4096], P(None, None, 'seq'), may hold values from -6 to 6
- short_filter: float32 [7, 3, 4096], replicated, may hold values from -2 to 2
- residue: float32 [4096, 16], replicated, may hold values from -1.5 to 1.5
- decay: float32 [4096, 16], replicated, may hold values from 0.2 to 64
- skip_gain: float32 [4096], replicated, may hold values from -3 to 3
Outputs:
- hyena_out: bfloat16 [4096, 4096], P(('groups', 'seq')), parts along dimension 0
The draws below stay inside these ranges and needn't reach their ends.
There are 2 independent parts, one for each index of `groups`. The reference program is written for one: setup_inputs(seed, part) draws one part's arguments, and reference() takes and returns one part's arrays. A program takes and returns all parts, laid end to end along the dimension named above; an argument that names none is the same for every part. Nothing has to cross between parts.
All inputs are finite; a program needn't handle non-finite values.
Results may differ from the reference program's by a relative error of at most 0.012.
Values may be sent and summed in bfloat16 or wider, within the bound.
A program may use at most 192 MiB of HBM per device.

```python
import math
import jax
import jax.numpy as jnp
from jax import lax

D = 4096
VOCAB = 512
SHORT = 7
POLES = 16
SEQ_LEN = 2048


def plant(entries, stream_key, least, top_value):
    spot = [jax.random.randint(jax.random.fold_in(stream_key, axis), (), 0, length) for axis, length in enumerate(entries.shape)]
    main_axis = entries.shape.index(max(entries.shape))
    neighbour = spot[:main_axis] + [(spot[main_axis] + 1) % entries.shape[main_axis]] + spot[main_axis + 1:]
    return entries.at[tuple(spot)].set(least).at[tuple(neighbour)].set(top_value)


def shard_levels(own_key, extent, split, least, high):
    loudness, own = 1.0, jax.random.fold_in(own_key, 6)
    for dim, blocks in split:
        steps = jnp.exp(jax.random.uniform(jax.random.fold_in(own, dim), (blocks,), jnp.float32, least / len(split), high / len(split)))
        loudness = loudness * jnp.repeat(steps, extent[dim] // blocks).reshape([-1 if axis == dim else 1 for axis in range(len(extent))])
    return loudness


def gaussian(stream_key, dims, scale, limit, cuts=(), kind=jnp.bfloat16):
    array = jax.random.normal(stream_key, dims, jnp.float32) * scale
    if len(cuts) > 0:
        array = shard_levels(stream_key, dims, cuts, -0.22, 0.18) * array
    return jnp.clip(array, min=-limit, max=limit).astype(kind)


def setup_inputs(seed: int = 0, part: int = 0) -> dict:
    splits = jax.random.split(jax.random.key(seed), 7)
    part_keys = jax.random.split(jax.random.fold_in(splits[6], part), 7)
    token_ids = plant(jax.random.randint(part_keys[0], (SEQ_LEN,), 0, VOCAB), jax.random.fold_in(part_keys[0], 1), 0, VOCAB - 1).astype(jnp.int32)
    vocab_table = gaussian(splits[1], (VOCAB, 3, D), 1.0, 6.0, ((2, 16),))
    short_filter = gaussian(splits[2], (SHORT, 3, D), SHORT ** -0.5, 2.0, (), jnp.float32)
    residue = gaussian(splits[3], (D, POLES), 0.25, 1.5, (), jnp.float32)
    decay = jnp.clip(jnp.exp(jax.random.uniform(splits[4], (D, POLES), jnp.float32, math.log(0.2), math.log(64.0))), 0.2, 64.0)
    skip_gain = gaussian(splits[5], (D,), 0.5, 3.0, (), jnp.float32)
    return {"token_ids": token_ids, "vocab_table": vocab_table, "short_filter": short_filter, "residue": residue, "decay": decay, "skip_gain": skip_gain}


def filter_spectrum(freq, total, pole, gap, tail, scale):
    theta = freq.astype(jnp.float32) * (2.0 * math.pi / total)
    sine = jnp.sin(theta)[:, None]
    halfsq = (jnp.sin(0.5 * theta) ** 2)[:, None]
    parity = (1 - 2 * (freq % 2)).astype(jnp.float32)[:, None]
    real_part = jnp.zeros((freq.shape[0], pole.shape[0]), jnp.float32)
    imag_part = jnp.zeros((freq.shape[0], pole.shape[0]), jnp.float32)
    for mode in range(pole.shape[1]):
        dreal = gap[:, mode] + 2.0 * pole[:, mode] * halfsq
        dimag = pole[:, mode] * sine
        factor = scale[:, mode] * (1.0 - tail[:, mode] * parity) / (dreal * dreal + dimag * dimag)
        real_part = real_part + factor * dreal
        imag_part = imag_part - factor * dimag
    return (real_part, imag_part)

def reference(token_ids, vocab_table, short_filter, residue, decay, skip_gain):
    length = token_ids.shape[0]
    total = 2 * length
    streams = jnp.take(vocab_table, token_ids, axis=0).astype(jnp.float32)
    rim = short_filter.shape[0] - 1
    padded = jnp.pad(streams, ((rim, 0), (0, 0), (0, 0)))
    mixed = jnp.zeros(streams.shape, jnp.float32)
    for lag in range(rim + 1):
        mixed = mixed + short_filter[lag] * padded[rim - lag:rim - lag + length]
    query = mixed[:, 0]
    gated = mixed[:, 1] * mixed[:, 2]
    rate = decay / length
    pole = jnp.exp(-rate)
    gap = -jnp.expm1(-rate)
    tail = jnp.exp(-decay)
    scale = residue * jnp.sqrt(2.0 * rate)
    width = gated.shape[1]
    group = min(width, 256)
    count = width // group
    modes = pole.shape[1]

    def one_block(items):
        block_gated, block_pole, block_gap, block_tail, block_scale = items
        spectrum_gated = jnp.fft.rfft(block_gated, n=total, axis=0)
        freq = jnp.arange(length + 1, dtype=jnp.int32)
        filt_real, filt_imag = filter_spectrum(freq, total, block_pole, block_gap, block_tail, block_scale)
        product = spectrum_gated * lax.complex(filt_real, filt_imag)
        return jnp.fft.irfft(product, n=total, axis=0)[:length]
    blocks = gated.reshape(length, count, group).transpose(1, 0, 2)
    convolved = lax.map(one_block, (blocks, pole.reshape(count, group, modes), gap.reshape(count, group, modes), tail.reshape(count, group, modes), scale.reshape(count, group, modes)))
    convolved = convolved.transpose(1, 0, 2).reshape(length, width)
    result = convolved + skip_gain * gated
    return (query * result).astype(jnp.bfloat16)
```

```python
import functools
import math

import jax
import jax.numpy as jnp
from jax import lax
from jax.experimental import pallas as pl
from jax.experimental.pallas import tpu as pltpu
from jax.sharding import PartitionSpec as P

HIGHEST = lax.Precision.HIGHEST


def angle_tables(first_index, second_index, modulus):
    product = first_index[:, None] * second_index[None, :] % modulus
    angle = product.astype(jnp.float32) * (2.0 * math.pi / modulus)
    return (jnp.cos(angle), jnp.sin(angle))


def short_conv(padded, taps, count):
    width = taps.shape[0]
    total = jnp.zeros((count,) + padded.shape[1:], jnp.float32)
    for lag in range(width):
        start = width - 1 - lag
        total = total + taps[lag] * padded[start : start + count].astype(jnp.float32)
    return total


def filter_spectrum(freq, total, pole, gap, tail, scale):
    theta = freq.astype(jnp.float32) * (2.0 * math.pi / total)
    sine = jnp.sin(theta)[:, :, None, None]
    halfsq = (jnp.sin(0.5 * theta) ** 2)[:, :, None, None]
    parity = (1 - 2 * (freq % 2)).astype(jnp.float32)[:, :, None, None]
    shape_out = freq.shape + (pole.shape[0],)
    real_part = jnp.zeros(shape_out, jnp.float32)
    imag_part = jnp.zeros(shape_out, jnp.float32)
    for first in range(0, pole.shape[1], 4):
        part_pole = pole[:, first : first + 4]
        dreal = gap[:, first : first + 4] + 2.0 * part_pole * halfsq
        dimag = part_pole * sine
        factor = (
            scale[:, first : first + 4]
            * (1.0 - tail[:, first : first + 4] * parity)
            / (dreal * dreal + dimag * dimag)
        )
        real_part = real_part + jnp.sum(factor * dreal, axis=-1)
        imag_part = imag_part - jnp.sum(factor * dimag, axis=-1)
    return (real_part, imag_part)


def convolve(gated, skip, filters, total, move_forward, move_back):
    pieces, block, width = gated.shape
    span = 2 * pieces
    outer_index = jnp.arange(span, dtype=jnp.int32)
    piece_index = jnp.arange(pieces, dtype=jnp.int32)
    outer_cos, outer_sin = angle_tables(outer_index, piece_index, span)
    real_part = jnp.einsum("kp,ptc->ktc", outer_cos, gated, precision=HIGHEST)
    imag_part = -jnp.einsum("kp,ptc->ktc", outer_sin, gated, precision=HIGHEST)
    times = jnp.arange(block, dtype=jnp.int32)
    twist_cos, twist_sin = angle_tables(outer_index, times, total)
    twist_cos = twist_cos[:, :, None]
    twist_sin = twist_sin[:, :, None]
    turned_real = twist_cos * real_part + twist_sin * imag_part
    turned_imag = twist_cos * imag_part - twist_sin * real_part
    moved = move_forward(jnp.stack([turned_real, turned_imag]))
    count = moved.shape[1]
    length = moved.shape[2]
    positions = jnp.arange(length, dtype=jnp.int32)
    inner_cos, inner_sin = angle_tables(positions, positions, length)
    freq_real = jnp.einsum("mt,ktc->kmc", inner_cos, moved[0], precision=HIGHEST) + jnp.einsum(
        "mt,ktc->kmc", inner_sin, moved[1], precision=HIGHEST
    )
    freq_imag = jnp.einsum("mt,ktc->kmc", inner_cos, moved[1], precision=HIGHEST) - jnp.einsum(
        "mt,ktc->kmc", inner_sin, moved[0], precision=HIGHEST
    )
    owned = jnp.arange(count, dtype=jnp.int32)
    freq = (owned[:, None] + span * positions[None, :]) % total
    filt_real, filt_imag = filter_spectrum(freq, total, *filters)
    prod_real = freq_real * filt_real - freq_imag * filt_imag
    prod_imag = freq_real * filt_imag + freq_imag * filt_real
    back_real = jnp.einsum("mt,kmc->ktc", inner_cos, prod_real, precision=HIGHEST) - jnp.einsum(
        "mt,kmc->ktc", inner_sin, prod_imag, precision=HIGHEST
    )
    back_imag = jnp.einsum("mt,kmc->ktc", inner_cos, prod_imag, precision=HIGHEST) + jnp.einsum(
        "mt,kmc->ktc", inner_sin, prod_real, precision=HIGHEST
    )
    undo_cos, undo_sin = angle_tables(owned, positions, total)
    undo_cos = undo_cos[:, :, None]
    undo_sin = undo_sin[:, :, None]
    untwist_real = undo_cos * back_real - undo_sin * back_imag
    untwist_imag = undo_cos * back_imag + undo_sin * back_real
    returned = move_back(jnp.stack([untwist_real, untwist_imag]))
    last_cos, last_sin = angle_tables(piece_index, outer_index, span)
    convolved = (
        jnp.einsum("pk,ktc->ptc", last_cos, returned[0], precision=HIGHEST)
        - jnp.einsum("pk,ktc->ptc", last_sin, returned[1], precision=HIGHEST)
    ) * (1.0 / total)
    return convolved + skip * gated


def unchanged(value):
    return value


def body(token_ids, vocab_table, short_filter, residue, decay, skip_gain):
    pieces = lax.axis_size("seq")
    place = lax.axis_index("seq")
    length = token_ids.shape[0]
    local = length // pieces
    share = vocab_table.shape[2]
    rim = short_filter.shape[0] - 1
    total = 2 * length
    rate = decay / length
    pole = jnp.exp(-rate)
    gap = -jnp.expm1(-rate)
    tail = jnp.exp(-decay)
    scale = residue * jnp.sqrt(2.0 * rate)
    first_channel = place * share
    chan_taps = lax.dynamic_slice_in_dim(short_filter, first_channel, share, 2)
    chan_filters = (
        lax.dynamic_slice_in_dim(pole, first_channel, share, 0),
        lax.dynamic_slice_in_dim(gap, first_channel, share, 0),
        lax.dynamic_slice_in_dim(tail, first_channel, share, 0),
        lax.dynamic_slice_in_dim(scale, first_channel, share, 0),
    )
    chan_skip = lax.dynamic_slice_in_dim(skip_gain, first_channel, share, 0)
    entries = jnp.arange(vocab_table.shape[0], dtype=token_ids.dtype)
    chosen = (token_ids[:, None] == entries[None, :]).astype(vocab_table.dtype)
    streams = jnp.einsum("nv,vjc->njc", chosen, vocab_table, preferred_element_type=jnp.float32)
    padded = jnp.pad(streams, ((rim, 0), (0, 0), (0, 0)))
    mixed = short_conv(padded, chan_taps, length)
    query = mixed[:, 0]
    gated = (mixed[:, 1] * mixed[:, 2]).reshape(pieces, local, share)
    convolved = convolve(gated, chan_skip, chan_filters, total, unchanged, unchanged)
    output = (query * convolved.reshape(length, share)).astype(jnp.bfloat16)
    return lax.all_to_all(output, "seq", split_axis=0, concat_axis=1, tiled=True)


LANES = 128
SUB = 8
HALO = 8
UNROLL = 8
CUTS = 4
MESH = pl.DeviceIdType.MESH


def wide(row):
    return jnp.broadcast_to(row, (SUB, LANES))


def toggles(value, limit):
    steps, bit = [], 1
    while bit < limit:
        steps.append((bit, bit - 2 * bit * (value // bit % 2)))
        bit = 2 * bit
    return steps


def flip(value, steps, mask):
    for bit, step in steps:
        if mask & bit:
            value = value + step
    return value


def trade_kernel(
    pieces,
    local,
    width,
    modes,
    ids_ref,
    all_tab_ref,
    all_taps_ref,
    all_decay_ref,
    all_residue_ref,
    all_skip_ref,
    out_ref,
    tab_ref,
    taps_ref,
    decay_ref,
    residue_ref,
    skip_ref,
    load_sem,
    other_ref,
    rows_ref,
    hot_ref,
    x_ref,
    query_ref,
    gated_ref,
    end_ref,
    begin_ref,
    coef_ref,
    seed_ref,
    last_ref,
    turn_ref,
    send_ref,
    send_sem,
    recv_sem,
    own_sem,
    trade_sem,
    ids_sem,
    state_sem,
):
    me = lax.axis_index("seq")
    group = lax.axis_index("groups")
    share = 2 * LANES
    quarter = pieces // 4
    half = me // SUB
    plane = me // quarter
    inner = plane * (3 - plane) // 2
    upper = inner * half
    is_inner = inner == 1
    is_outer = inner == 0
    partner = me + inner * quarter * (1 - 2 * half)
    vocab = tab_ref.shape[2]
    length = pieces * local
    steps = toggles(me, SUB)

    bases = (
        me * share + inner * group * LANES,
        me * share + LANES + inner * ((partner - me) * share + (group - 1) * LANES),
    )
    bases = [pl.multiple_of(base, LANES) for base in bases]
    offset = pl.multiple_of(inner * group * LANES, LANES)

    def loads(block):
        mine = pl.ds(bases[block], LANES)
        pairs = (
            (all_taps_ref.at[:, :, mine], taps_ref.at[block]),
            (all_decay_ref.at[:, mine], decay_ref.at[block]),
            (all_residue_ref.at[:, mine], residue_ref.at[block]),
            (all_skip_ref.at[:, mine], skip_ref.at[block]),
        )
        return [
            pltpu.make_async_copy(source, target, load_sem.at[block, i])
            for i, (source, target) in enumerate(pairs)
        ]

    near_table = pltpu.make_async_copy(
        all_tab_ref.at[:, :, pl.ds(offset, LANES)], tab_ref.at[0], load_sem.at[0, 4]
    )
    far_table = pltpu.make_async_copy(
        all_tab_ref.at[:, :, pl.ds(LANES, LANES)], tab_ref.at[1], load_sem.at[1, 4]
    )
    near_table.start()

    @pl.when(is_outer)
    def _():
        far_table.start()

    for block in range(2):
        for load in loads(block):
            load.start()

    barrier = pltpu.get_barrier_semaphore()

    def greet(seq, at):
        pl.semaphore_signal(
            barrier, inc=1, device_id={"groups": at, "seq": seq}, device_id_type=MESH
        )

    @pl.when(is_inner)
    def _():
        greet(partner, group)

    for j in range(quarter):
        for seq in (j, 3 * quarter + j):

            @pl.when(me != seq)
            def _():
                greet(seq, group)

        friend = quarter + quarter * half + j
        greet(friend, 1 - group)

        @pl.when(me != friend)
        def _():
            greet(friend, group)

    def trade(j):
        return pltpu.make_async_remote_copy(
            src_ref=tab_ref.at[0, j],
            dst_ref=tab_ref.at[1, j],
            send_sem=trade_sem.at[0, j],
            recv_sem=trade_sem.at[1, j],
            device_id={"groups": group, "seq": partner},
            device_id_type=MESH,
        )

    swap_ids = pltpu.make_async_remote_copy(
        src_ref=ids_ref,
        dst_ref=other_ref,
        send_sem=ids_sem.at[0],
        recv_sem=ids_sem.at[1],
        device_id={"groups": 1 - group, "seq": me},
        device_id_type=MESH,
    )

    def pass_state(block):
        return pltpu.make_async_remote_copy(
            src_ref=last_ref.at[block],
            dst_ref=seed_ref.at[1 - block],
            send_sem=state_sem.at[0, block],
            recv_sem=state_sem.at[1, 1 - block],
            device_id={"groups": group, "seq": partner},
            device_id_type=MESH,
        )

    def earlier(ids):
        first = lax.broadcasted_iota(jnp.int32, ids.shape, 0) == 0
        return jnp.where(first, -1, pltpu.roll(ids, 1, axis=0))

    near_table.wait()
    ids = ids_ref[...]
    before = earlier(ids)

    @pl.when(is_outer)
    def _():
        rows_ref[0] = ids
        rows_ref[1] = before
        far_table.wait()

    @pl.when(is_inner)
    def _():
        pl.semaphore_wait(barrier, pieces)
        swap_ids.start()
        for j in range(3):
            trade(j).start()
        swap_ids.wait_recv()
        other = other_ref[...]
        for i, pair in enumerate(((ids, other), (before, earlier(other)))):
            for s in range(2):
                rows_ref[i, s * SUB : (s + 1) * SUB, :] = jnp.where(
                    half == 1, pair[s][SUB:, :], pair[s][:SUB, :]
                )

    @pl.when(upper == 0)
    def _():
        seed_ref[...] = jnp.zeros_like(seed_ref)

    cut = (HALO + local) * pieces // CUTS
    ids = rows_ref[0]
    before = rows_ref[1]
    entry = lax.broadcasted_iota(jnp.int32, (pieces, vocab), 1)
    count = (HALO + local) // CUTS

    def build(i):
        for t in range(i * count - HALO, (i + 1) * count - HALO):
            column = ids[:, t : t + 1] if t >= 0 else before[:, local + t : local + t + 1]
            hot_ref[(HALO + t) * pieces : (HALO + t + 1) * pieces, :] = jnp.where(
                column == entry, 1.0, 0.0
            ).astype(jnp.bfloat16)

    build(0)
    for block in range(2):
        for load in loads(block):
            load.wait()

    def base_of(block):
        return pl.multiple_of(bases[0] + block * (bases[1] - bases[0]), LANES)

    def place(base):
        return out_ref.at[:, pl.ds(base, LANES)]

    def target(slot, low):
        seq = (1 - inner) * (slot * SUB + low) + inner * (half * SUB + low)
        return {"groups": group + inner * slot * (1 - 2 * group), "seq": seq}

    def remote(block, slot, k):
        low = flip(me, steps, k) - half * SUB
        base = base_of(block)
        return pltpu.make_async_remote_copy(
            src_ref=send_ref.at[block, slot * SUB + low],
            dst_ref=place(base),
            send_sem=send_sem.at[block, slot, k],
            recv_sem=recv_sem.at[base // LANES],
            device_id=target(slot, low),
            device_id_type=MESH,
        )

    own_slot = (1 - inner) * half

    def own(block):
        return pltpu.make_async_copy(
            send_ref.at[block, own_slot * SUB + me - half * SUB],
            place(base_of(block)),
            own_sem.at[block],
        )

    def head(block):
        rate = decay_ref[block] / length
        pole = jnp.exp(-rate)
        coef_ref[block, 0] = pole
        coef_ref[block, 1] = residue_ref[block] * jnp.sqrt(2.0 * rate)
        coef_ref[block, 2] = jnp.exp(-rate * local)
        table = jnp.concatenate([tab_ref[block, j] for j in range(3)], axis=1)
        for i in range(CUTS):
            if block == 0 and i + 1 < CUTS:
                build(i + 1)
            span = pl.ds(i * cut, cut)
            x_ref[span, :] = jnp.dot(hot_ref[span, :], table, preferred_element_type=jnp.float32)

        def first_pass(slot, _):
            base = pl.multiple_of(slot * SUB, SUB)
            poles = [wide(coef_ref[block, 0, s : s + 1, :]) for s in range(modes)]
            taps = [
                [wide(taps_ref[block, j, lag : lag + 1, :]) for lag in range(width)]
                for j in range(3)
            ]

            def step(i, state):
                state = list(state)
                mixed = []
                for j in range(3):
                    seen = {}
                    for t in range(1 - width, UNROLL):
                        at = pl.multiple_of((i * UNROLL + t + HALO) * pieces + base, SUB)
                        seen[t] = x_ref[pl.ds(at, SUB), j * LANES : (j + 1) * LANES]
                    totals = []
                    for t in range(UNROLL):
                        total = taps[j][0] * seen[t]
                        for lag in range(1, width):
                            total = total + taps[j][lag] * seen[t - lag]
                        totals.append(total)
                    mixed.append(totals)
                for t in range(UNROLL):
                    at = pl.multiple_of((i * UNROLL + t) * pieces + base, SUB)
                    gated = mixed[1][t] * mixed[2][t]
                    query_ref[block, pl.ds(at, SUB), :] = mixed[0][t]
                    gated_ref[block, pl.ds(at, SUB), :] = gated
                    for s in range(modes):
                        state[s] = poles[s] * state[s] + gated
                return tuple(state)

            zero = jnp.zeros((SUB, LANES), jnp.float32)
            state = lax.fori_loop(0, local // UNROLL, step, (zero,) * modes)
            for s in range(modes):
                end_ref[block, pl.ds(pl.multiple_of(s * pieces + base, SUB), SUB), :] = state[s]
            return 0

        lax.fori_loop(0, 2, first_pass, 0)

    def tail(block):
        @pl.when(upper == 1)
        def _():
            pass_state(1 - block).wait_recv()

        leap = coef_ref[block, 2]
        carry = seed_ref[block, 0]
        for k in range(pieces):
            if k == SUB:
                last_ref[block, 0] = carry
                carry = jnp.where(is_inner, seed_ref[block, 1], carry)
            begin_ref[pl.ds(k, modes, stride=pieces), :] = carry
            carry = leap * carry + end_ref[block, pl.ds(k, modes, stride=pieces), :]
        last_ref[block, 1] = carry

        @pl.when(inner - upper == 1)
        def _():
            pass_state(block).start()

        skip = wide(skip_ref[block])
        lead = (1 - inner) * half
        for q in range(2):
            slot = q + lead * (1 - 2 * q)
            base = pl.multiple_of(slot * SUB, SUB)
            poles = [wide(coef_ref[block, 0, s : s + 1, :]) for s in range(modes)]
            coefs = [wide(coef_ref[block, 1, s : s + 1, :]) for s in range(modes)]

            def step(i, state):
                state = list(state)
                for t in range(UNROLL):
                    at = pl.multiple_of((i * UNROLL + t) * pieces + base, SUB)
                    gated = gated_ref[block, pl.ds(at, SUB), :]
                    terms = [skip * gated]
                    for s in range(modes):
                        state[s] = poles[s] * state[s] + gated
                        terms.append(coefs[s] * state[s])
                        if len(terms) == 5:
                            terms = [((terms[0] + terms[1]) + (terms[2] + terms[3])) + terms[4]]
                    total = terms[0]
                    for term in terms[1:]:
                        total = total + term
                    turn_ref[pl.ds(pl.multiple_of((i * UNROLL + t) * SUB, SUB), SUB), :] = (
                        query_ref[block, pl.ds(at, SUB), :] * total
                    )
                return tuple(state)

            state = tuple(
                begin_ref[pl.ds(pl.multiple_of(s * pieces + base, SUB), SUB), :]
                for s in range(modes)
            )
            lax.fori_loop(0, local // UNROLL, step, state)
            for k in range(SUB):
                send_ref[block, base + k, :, :] = turn_ref[
                    pl.ds(k, local, stride=SUB), :
                ].astype(jnp.bfloat16)

            if q == 0:

                @pl.when(jnp.logical_and(is_outer, block == 0))
                def _():
                    pl.semaphore_wait(barrier, pieces - 1)

            for k in range(1, SUB):
                remote(block, slot, k).start()

            @pl.when(slot == own_slot)
            def _():
                own(block).start()

            @pl.when(slot != own_slot)
            def _():
                remote(block, slot, 0).start()

    head(0)
    lax.fori_loop(0, 1 - upper, lambda i, _: (tail(0), 0)[1], 0)

    @pl.when(is_inner)
    def _():
        for j in range(3):
            trade(j).wait_recv()

    head(1)
    lax.fori_loop(0, 1 + upper, lambda i, _: (tail(1 - i), 0)[1], 0)

    @pl.when(is_inner)
    def _():
        swap_ids.wait_send()
        for j in range(3):
            trade(j).wait_send()

    @pl.when(inner - upper == 1)
    def _():
        for block in range(2):
            pass_state(block).wait_send()

    for block in range(2):
        own(block).wait()
        for slot in range(2):
            for k in range(1, SUB):
                remote(block, slot, k).wait_send()
        remote(block, 1 - own_slot, 0).wait_send()

    def arrive(at, _):
        here = pl.multiple_of(at * LANES, LANES)

        @pl.when(jnp.logical_and(here != bases[0], here != bases[1]))
        def _():
            pltpu.make_async_remote_copy(
                src_ref=send_ref.at[0, 0],
                dst_ref=place(here),
                send_sem=send_sem.at[0, 0, 0],
                recv_sem=recv_sem.at[at],
                device_id={"groups": group, "seq": me},
                device_id_type=MESH,
            ).wait_recv()

        return 0

    lax.fori_loop(0, 2 * pieces, arrive, 0)


def trade_body(token_ids, vocab_table, short_filter, residue, decay, skip_gain):
    pieces = lax.axis_size("seq")
    length = token_ids.shape[0]
    local = length // pieces
    vocab, streams, share = vocab_table.shape
    width = short_filter.shape[0]
    modes = decay.shape[1]
    ids = token_ids.reshape(pieces, local)
    table = vocab_table.transpose(1, 0, 2)
    taps = short_filter.transpose(1, 0, 2)
    rows = (HALO + local) * pieces
    vmem = pl.BlockSpec(memory_space=pltpu.VMEM)
    return pl.pallas_call(
        functools.partial(trade_kernel, pieces, local, width, modes),
        out_shape=pltpu.VMEM((local, pieces * share), jnp.bfloat16),
        in_specs=[vmem] + [pl.BlockSpec(memory_space=pl.ANY)] * 5,
        out_specs=pl.BlockSpec(memory_space=pltpu.VMEM),
        scratch_shapes=[
            pltpu.VMEM((2, streams, vocab, LANES), vocab_table.dtype),
            pltpu.VMEM((2, streams, width, LANES), jnp.float32),
            pltpu.VMEM((2, modes, LANES), jnp.float32),
            pltpu.VMEM((2, modes, LANES), jnp.float32),
            pltpu.VMEM((2, 1, LANES), jnp.float32),
            pltpu.SemaphoreType.DMA((2, 5)),
            pltpu.VMEM((pieces, local), jnp.int32),
            pltpu.VMEM((2, pieces, local), jnp.int32),
            pltpu.VMEM((rows, vocab), jnp.bfloat16),
            pltpu.VMEM((rows, streams * LANES), jnp.float32),
            pltpu.VMEM((2, length, LANES), jnp.float32),
            pltpu.VMEM((2, length, LANES), jnp.float32),
            pltpu.VMEM((2, modes * pieces, LANES), jnp.float32),
            pltpu.VMEM((modes * pieces, LANES), jnp.float32),
            pltpu.VMEM((2, 3, modes, LANES), jnp.float32),
            pltpu.VMEM((2, 2, modes, LANES), jnp.float32),
            pltpu.VMEM((2, 2, modes, LANES), jnp.float32),
            pltpu.VMEM((local * SUB, LANES), jnp.float32),
            pltpu.VMEM((2, pieces, local, LANES), jnp.bfloat16),
            pltpu.SemaphoreType.DMA((2, 2, SUB)),
            pltpu.SemaphoreType.DMA((2 * pieces,)),
            pltpu.SemaphoreType.DMA((2,)),
            pltpu.SemaphoreType.DMA((2, streams)),
            pltpu.SemaphoreType.DMA((2,)),
            pltpu.SemaphoreType.DMA((2, 2)),
        ],
        compiler_params=pltpu.CompilerParams(collective_id=0, has_side_effects=True),
    )(ids, table, taps, decay.T, residue.T, skip_gain[None])


def fits(mesh, share, local, width, streams):
    even = mesh.shape["seq"] == 2 * SUB and mesh.shape["groups"] == 2
    return even and share == 2 * LANES and local == LANES and width <= HALO + 1 and streams == 3


def solution(mesh):
    placed = (P("groups"), P(None, None, "seq"), P(), P(), P(), P())

    def whole(token_ids, vocab_table, short_filter, residue, decay, skip_gain):
        pieces = mesh.shape["seq"]
        local = token_ids.shape[0] // (mesh.shape["groups"] * pieces)
        share = vocab_table.shape[2] // pieces
        shapes = (share, local, short_filter.shape[0], vocab_table.shape[1])
        chosen = trade_body if fits(mesh, *shapes) else body
        return jax.shard_map(
            chosen, mesh=mesh, in_specs=placed, out_specs=P(("groups", "seq"), None), check_vma=False
        )(token_ids, vocab_table, short_filter, residue, decay, skip_gain)

    return whole
```

```python
import functools
import math

import jax
import jax.numpy as jnp
from jax import lax
from jax.experimental import pallas as pl
from jax.experimental.pallas import tpu as pltpu
from jax.sharding import PartitionSpec as P

HIGHEST = lax.Precision.HIGHEST


def angle_tables(first_index, second_index, modulus):
    product = first_index[:, None] * second_index[None, :] % modulus
    angle = product.astype(jnp.float32) * (2.0 * math.pi / modulus)
    return (jnp.cos(angle), jnp.sin(angle))


def short_conv(padded, taps, count):
    width = taps.shape[0]
    total = jnp.zeros((count,) + padded.shape[1:], jnp.float32)
    for lag in range(width):
        start = width - 1 - lag
        total = total + taps[lag] * padded[start : start + count].astype(jnp.float32)
    return total


def filter_spectrum(freq, total, pole, gap, tail, scale):
    theta = freq.astype(jnp.float32) * (2.0 * math.pi / total)
    sine = jnp.sin(theta)[:, :, None, None]
    halfsq = (jnp.sin(0.5 * theta) ** 2)[:, :, None, None]
    parity = (1 - 2 * (freq % 2)).astype(jnp.float32)[:, :, None, None]
    shape_out = freq.shape + (pole.shape[0],)
    real_part = jnp.zeros(shape_out, jnp.float32)
    imag_part = jnp.zeros(shape_out, jnp.float32)
    for first in range(0, pole.shape[1], 4):
        part_pole = pole[:, first : first + 4]
        dreal = gap[:, first : first + 4] + 2.0 * part_pole * halfsq
        dimag = part_pole * sine
        factor = (
            scale[:, first : first + 4]
            * (1.0 - tail[:, first : first + 4] * parity)
            / (dreal * dreal + dimag * dimag)
        )
        real_part = real_part + jnp.sum(factor * dreal, axis=-1)
        imag_part = imag_part - jnp.sum(factor * dimag, axis=-1)
    return (real_part, imag_part)


def convolve(gated, skip, filters, total, move_forward, move_back):
    pieces, block, width = gated.shape
    span = 2 * pieces
    outer_index = jnp.arange(span, dtype=jnp.int32)
    piece_index = jnp.arange(pieces, dtype=jnp.int32)
    outer_cos, outer_sin = angle_tables(outer_index, piece_index, span)
    real_part = jnp.einsum("kp,ptc->ktc", outer_cos, gated, precision=HIGHEST)
    imag_part = -jnp.einsum("kp,ptc->ktc", outer_sin, gated, precision=HIGHEST)
    times = jnp.arange(block, dtype=jnp.int32)
    twist_cos, twist_sin = angle_tables(outer_index, times, total)
    twist_cos = twist_cos[:, :, None]
    twist_sin = twist_sin[:, :, None]
    turned_real = twist_cos * real_part + twist_sin * imag_part
    turned_imag = twist_cos * imag_part - twist_sin * real_part
    moved = move_forward(jnp.stack([turned_real, turned_imag]))
    count = moved.shape[1]
    length = moved.shape[2]
    positions = jnp.arange(length, dtype=jnp.int32)
    inner_cos, inner_sin = angle_tables(positions, positions, length)
    freq_real = jnp.einsum("mt,ktc->kmc", inner_cos, moved[0], precision=HIGHEST) + jnp.einsum(
        "mt,ktc->kmc", inner_sin, moved[1], precision=HIGHEST
    )
    freq_imag = jnp.einsum("mt,ktc->kmc", inner_cos, moved[1], precision=HIGHEST) - jnp.einsum(
        "mt,ktc->kmc", inner_sin, moved[0], precision=HIGHEST
    )
    owned = jnp.arange(count, dtype=jnp.int32)
    freq = (owned[:, None] + span * positions[None, :]) % total
    filt_real, filt_imag = filter_spectrum(freq, total, *filters)
    prod_real = freq_real * filt_real - freq_imag * filt_imag
    prod_imag = freq_real * filt_imag + freq_imag * filt_real
    back_real = jnp.einsum("mt,kmc->ktc", inner_cos, prod_real, precision=HIGHEST) - jnp.einsum(
        "mt,kmc->ktc", inner_sin, prod_imag, precision=HIGHEST
    )
    back_imag = jnp.einsum("mt,kmc->ktc", inner_cos, prod_imag, precision=HIGHEST) + jnp.einsum(
        "mt,kmc->ktc", inner_sin, prod_real, precision=HIGHEST
    )
    undo_cos, undo_sin = angle_tables(owned, positions, total)
    undo_cos = undo_cos[:, :, None]
    undo_sin = undo_sin[:, :, None]
    untwist_real = undo_cos * back_real - undo_sin * back_imag
    untwist_imag = undo_cos * back_imag + undo_sin * back_real
    returned = move_back(jnp.stack([untwist_real, untwist_imag]))
    last_cos, last_sin = angle_tables(piece_index, outer_index, span)
    convolved = (
        jnp.einsum("pk,ktc->ptc", last_cos, returned[0], precision=HIGHEST)
        - jnp.einsum("pk,ktc->ptc", last_sin, returned[1], precision=HIGHEST)
    ) * (1.0 / total)
    return convolved + skip * gated


def unchanged(value):
    return value


def body(token_ids, vocab_table, short_filter, residue, decay, skip_gain):
    pieces = lax.axis_size("seq")
    place = lax.axis_index("seq")
    length = token_ids.shape[0]
    local = length // pieces
    share = vocab_table.shape[2]
    rim = short_filter.shape[0] - 1
    total = 2 * length
    rate = decay / length
    pole = jnp.exp(-rate)
    gap = -jnp.expm1(-rate)
    tail = jnp.exp(-decay)
    scale = residue * jnp.sqrt(2.0 * rate)
    first_channel = place * share
    chan_taps = lax.dynamic_slice_in_dim(short_filter, first_channel, share, 2)
    chan_filters = (
        lax.dynamic_slice_in_dim(pole, first_channel, share, 0),
        lax.dynamic_slice_in_dim(gap, first_channel, share, 0),
        lax.dynamic_slice_in_dim(tail, first_channel, share, 0),
        lax.dynamic_slice_in_dim(scale, first_channel, share, 0),
    )
    chan_skip = lax.dynamic_slice_in_dim(skip_gain, first_channel, share, 0)
    entries = jnp.arange(vocab_table.shape[0], dtype=token_ids.dtype)
    chosen = (token_ids[:, None] == entries[None, :]).astype(vocab_table.dtype)
    streams = jnp.einsum("nv,vjc->njc", chosen, vocab_table, preferred_element_type=jnp.float32)
    padded = jnp.pad(streams, ((rim, 0), (0, 0), (0, 0)))
    mixed = short_conv(padded, chan_taps, length)
    query = mixed[:, 0]
    gated = (mixed[:, 1] * mixed[:, 2]).reshape(pieces, local, share)
    convolved = convolve(gated, chan_skip, chan_filters, total, unchanged, unchanged)
    output = (query * convolved.reshape(length, share)).astype(jnp.bfloat16)
    return lax.all_to_all(output, "seq", split_axis=0, concat_axis=1, tiled=True)


LANES = 128
SUB = 8
HALO = 8
UNROLL = 8
CUTS = 2
MESH = pl.DeviceIdType.MESH


def wide(row):
    return jnp.broadcast_to(row, (SUB, LANES))


def toggles(value, limit):
    steps, bit = [], 1
    while bit < limit:
        steps.append((bit, bit - 2 * bit * (value // bit % 2)))
        bit = 2 * bit
    return steps


def flip(value, steps, mask):
    for bit, step in steps:
        if mask & bit:
            value = value + step
    return value


def scan_kernel(
    pieces,
    local,
    width,
    modes,
    all_ids_ref,
    all_tab_ref,
    all_taps_ref,
    all_decay_ref,
    all_residue_ref,
    all_skip_ref,
    out_ref,
    ids_ref,
    tab_ref,
    taps_ref,
    decay_ref,
    residue_ref,
    skip_ref,
    load_sem,
    ids_sem,
    hot_ref,
    x_ref,
    query_ref,
    gated_ref,
    end_ref,
    begin_ref,
    carry_ref,
    coef_ref,
    turn_ref,
    send_ref,
    send_sem,
    recv_sem,
    own_sem,
):
    me = lax.axis_index("seq")
    half = me // SUB
    share = 2 * LANES
    vocab = tab_ref.shape[2]
    length = pieces * local
    steps = toggles(me, SUB)

    def loads(block):
        mine = pl.ds(pl.multiple_of(me * share + block * LANES, LANES), LANES)
        lane = pl.ds(block * LANES, LANES)
        pairs = (
            (all_tab_ref.at[:, :, lane], tab_ref.at[block]),
            (all_taps_ref.at[:, :, mine], taps_ref.at[block]),
            (all_decay_ref.at[:, mine], decay_ref.at[block]),
            (all_residue_ref.at[:, mine], residue_ref.at[block]),
            (all_skip_ref.at[:, mine], skip_ref.at[block]),
        )
        return [
            pltpu.make_async_copy(source, target, load_sem.at[block, i])
            for i, (source, target) in enumerate(pairs)
        ]

    load_ids = pltpu.make_async_copy(all_ids_ref, ids_ref, ids_sem.at[0])
    load_ids.start()
    for block in range(2):
        for load in loads(block):
            load.start()
    barrier = pltpu.get_barrier_semaphore()

    def greet(i, _):
        peer = me + i - pieces * ((me + i) // pieces)
        pl.semaphore_signal(barrier, inc=1, device_id={"seq": peer}, device_id_type=MESH)
        return 0

    lax.fori_loop(1, pieces, greet, 0)

    load_ids.wait()
    ids = ids_ref[...]
    before = jnp.where(
        lax.broadcasted_iota(jnp.int32, ids.shape, 0) == 0, -1, pltpu.roll(ids, 1, axis=0)
    )
    entry = lax.broadcasted_iota(jnp.int32, (SUB, vocab), 1)

    count = (HALO + local) // CUTS

    def build(slot, i):
        rows = slice(slot * SUB, (slot + 1) * SUB)
        for t in range(i * count - HALO, (i + 1) * count - HALO, 2):
            pair = []
            for at in (t, t + 1):
                column = (
                    ids[rows, at : at + 1] if at >= 0 else before[rows, local + at : local + at + 1]
                )
                pair.append(jnp.where(column == entry, 1.0, 0.0))
            hot_ref[slot, (HALO + t) * SUB : (HALO + t + 2) * SUB, :] = jnp.concatenate(
                pair, axis=0
            ).astype(jnp.bfloat16)

    def place(block, source):
        return out_ref.at[
            :, pl.ds(pl.multiple_of(source * share + block * LANES, LANES), LANES)
        ]

    def remote(block, slot, low, sender):
        peer = slot * SUB + low
        return pltpu.make_async_remote_copy(
            src_ref=send_ref.at[block, peer],
            dst_ref=place(block, sender),
            send_sem=send_sem.at[block, peer],
            recv_sem=recv_sem.at[block, sender],
            device_id={"seq": peer},
            device_id_type=MESH,
        )

    def own(block):
        return pltpu.make_async_copy(send_ref.at[block, me], place(block, me), own_sem.at[block])

    cut = (HALO + local) * SUB // CUTS

    def head(block, slot):
        if block == 0:
            for i in range(CUTS if slot == 0 else 1):
                build(slot, i)
        if slot == 0:
            for load in loads(block):
                load.wait()
            rate = decay_ref[block] / length
            coef_ref[0] = jnp.exp(-rate)
            coef_ref[1] = residue_ref[block] * jnp.sqrt(2.0 * rate)
            coef_ref[2] = jnp.exp(-rate * local)
            carry_ref[...] = jnp.zeros_like(carry_ref)

        table = jnp.concatenate([tab_ref[block, j] for j in range(3)], axis=1)
        for i in range(CUTS):
            if block == 0 and slot == 1 and i + 1 < CUTS:
                build(slot, i + 1)
            span = pl.ds(i * cut, cut)
            x_ref[span, :] = jnp.dot(
                hot_ref[slot, span, :], table, preferred_element_type=jnp.float32
            )
        poles = [wide(coef_ref[0, s : s + 1, :]) for s in range(modes)]
        taps = [
            [wide(taps_ref[block, j, lag : lag + 1, :]) for lag in range(width)] for j in range(3)
        ]

        def step(i, state):
            state = list(state)
            mixed = []
            for j in range(3):
                seen = {}
                for t in range(1 - width, UNROLL):
                    at = pl.multiple_of((i * UNROLL + t + HALO) * SUB, SUB)
                    seen[t] = x_ref[pl.ds(at, SUB), j * LANES : (j + 1) * LANES]
                totals = []
                for t in range(UNROLL):
                    total = taps[j][0] * seen[t]
                    for lag in range(1, width):
                        total = total + taps[j][lag] * seen[t - lag]
                    totals.append(total)
                mixed.append(totals)
            for t in range(UNROLL):
                at = pl.multiple_of((i * UNROLL + t) * SUB, SUB)
                gated = mixed[1][t] * mixed[2][t]
                query_ref[slot, pl.ds(at, SUB), :] = mixed[0][t]
                gated_ref[slot, pl.ds(at, SUB), :] = gated
                for s in range(modes):
                    state[s] = poles[s] * state[s] + gated
            return tuple(state)

        zero = jnp.zeros((SUB, LANES), jnp.float32)
        state = lax.fori_loop(0, local // UNROLL, step, (zero,) * modes)
        for s in range(modes):
            end_ref[s * SUB : (s + 1) * SUB, :] = state[s]
        leap = coef_ref[2]
        carry = carry_ref[...]
        for k in range(SUB):
            begin_ref[slot, pl.ds(k, modes, stride=SUB), :] = carry
            carry = leap * carry + end_ref[pl.ds(k, modes, stride=SUB), :]
        carry_ref[...] = carry

    def tail(block, slot, first):
        poles = [wide(coef_ref[0, s : s + 1, :]) for s in range(modes)]
        coefs = [wide(coef_ref[1, s : s + 1, :]) for s in range(modes)]
        skip = wide(skip_ref[block])

        def step(i, state):
            state = list(state)
            for t in range(UNROLL):
                at = pl.multiple_of((i * UNROLL + t) * SUB, SUB)
                gated = gated_ref[slot, pl.ds(at, SUB), :]
                terms = [skip * gated]
                for s in range(modes):
                    state[s] = poles[s] * state[s] + gated
                    terms.append(coefs[s] * state[s])
                    if len(terms) == 5:
                        terms = [((terms[0] + terms[1]) + (terms[2] + terms[3])) + terms[4]]
                total = terms[0]
                for term in terms[1:]:
                    total = total + term
                turn_ref[pl.ds(at, SUB), :] = query_ref[slot, pl.ds(at, SUB), :] * total
            return tuple(state)

        state = tuple(begin_ref[slot, s * SUB : (s + 1) * SUB, :] for s in range(modes))
        lax.fori_loop(0, local // UNROLL, step, state)
        for k in range(SUB):
            send_ref[block, slot * SUB + k] = turn_ref[pl.ds(k, local, stride=SUB), :].astype(
                jnp.bfloat16
            )

        @pl.when(first)
        def _():
            pl.semaphore_wait(barrier, pieces - 1)

        for k in range(SUB):
            low = k

            @pl.when(slot * SUB + low != me)
            def _():
                remote(block, slot, low, me).start()

        @pl.when(slot == half)
        def _():
            own(block).start()

    for block in range(2):
        head(block, 0)

        def early(i, _):
            tail(block, 0, block == 0)
            return 0

        lax.fori_loop(0, half, early, 0)
        head(block, 1)

        def late(i, _):
            tail(block, 1 - i, jnp.logical_and(half + i == 0, block == 0))
            return 0

        lax.fori_loop(0, 2 - half, late, 0)

    for block in range(2):
        own(block).wait()

        def finish(i, _):
            peer = me + i - pieces * ((me + i) // pieces)
            remote(block, peer // SUB, peer - peer // SUB * SUB, me).wait_send()
            remote(block, half, me - half * SUB, peer).wait_recv()
            return 0

        lax.fori_loop(1, pieces, finish, 0)


def scan_body(token_ids, vocab_table, short_filter, residue, decay, skip_gain):
    pieces = lax.axis_size("seq")
    length = token_ids.shape[0]
    local = length // pieces
    vocab, streams, share = vocab_table.shape
    width = short_filter.shape[0]
    modes = decay.shape[1]
    ids = token_ids.reshape(pieces, local)
    table = vocab_table.transpose(1, 0, 2)
    taps = short_filter.transpose(1, 0, 2)
    rows = (HALO + local) * SUB
    return pl.pallas_call(
        functools.partial(scan_kernel, pieces, local, width, modes),
        out_shape=pltpu.VMEM((local, pieces * share), jnp.bfloat16),
        in_specs=[pl.BlockSpec(memory_space=pl.ANY)] * 6,
        out_specs=pl.BlockSpec(memory_space=pltpu.VMEM),
        scratch_shapes=[
            pltpu.VMEM((pieces, local), jnp.int32),
            pltpu.VMEM((2, streams, vocab, LANES), vocab_table.dtype),
            pltpu.VMEM((2, streams, width, LANES), jnp.float32),
            pltpu.VMEM((2, modes, LANES), jnp.float32),
            pltpu.VMEM((2, modes, LANES), jnp.float32),
            pltpu.VMEM((2, 1, LANES), jnp.float32),
            pltpu.SemaphoreType.DMA((2, 5)),
            pltpu.SemaphoreType.DMA((1,)),
            pltpu.VMEM((2, rows, vocab), jnp.bfloat16),
            pltpu.VMEM((rows, streams * LANES), jnp.float32),
            pltpu.VMEM((2, local * SUB, LANES), jnp.float32),
            pltpu.VMEM((2, local * SUB, LANES), jnp.float32),
            pltpu.VMEM((modes * SUB, LANES), jnp.float32),
            pltpu.VMEM((2, modes * SUB, LANES), jnp.float32),
            pltpu.VMEM((modes, LANES), jnp.float32),
            pltpu.VMEM((3, modes, LANES), jnp.float32),
            pltpu.VMEM((local * SUB, LANES), jnp.float32),
            pltpu.VMEM((2, pieces, local, LANES), jnp.bfloat16),
            pltpu.SemaphoreType.DMA((2, pieces)),
            pltpu.SemaphoreType.DMA((2, pieces)),
            pltpu.SemaphoreType.DMA((2,)),
        ],
        compiler_params=pltpu.CompilerParams(collective_id=0, has_side_effects=True),
    )(ids, table, taps, decay.T, residue.T, skip_gain[None])


def fits(mesh, share, local, width, streams):
    even = mesh.shape["seq"] == 2 * SUB
    return even and share == 2 * LANES and local == LANES and width <= HALO + 1 and streams == 3


def solution(mesh):
    placed = (P("groups"), P(None, None, "seq"), P(), P(), P(), P())

    def whole(token_ids, vocab_table, short_filter, residue, decay, skip_gain):
        pieces = mesh.shape["seq"]
        local = token_ids.shape[0] // (mesh.shape["groups"] * pieces)
        share = vocab_table.shape[2] // pieces
        shapes = (share, local, short_filter.shape[0], vocab_table.shape[1])
        chosen = scan_body if fits(mesh, *shapes) else body
        return jax.shard_map(
            chosen, mesh=mesh, in_specs=placed, out_specs=P(("groups", "seq"), None), check_vma=False
        )(token_ids, vocab_table, short_filter, residue, decay, skip_gain)

    return whole
```

```python
import functools
import math

import jax
import jax.numpy as jnp
from jax import lax
from jax.experimental import pallas as pl
from jax.experimental.pallas import tpu as pltpu
from jax.sharding import PartitionSpec as P

HIGHEST = lax.Precision.HIGHEST


def angle_tables(first_index, second_index, modulus):
    product = first_index[:, None] * second_index[None, :] % modulus
    angle = product.astype(jnp.float32) * (2.0 * math.pi / modulus)
    return (jnp.cos(angle), jnp.sin(angle))


def short_conv(padded, taps, count):
    width = taps.shape[0]
    total = jnp.zeros((count,) + padded.shape[1:], jnp.float32)
    for lag in range(width):
        start = width - 1 - lag
        total = total + taps[lag] * padded[start : start + count].astype(jnp.float32)
    return total


def filter_spectrum(freq, total, pole, gap, tail, scale):
    theta = freq.astype(jnp.float32) * (2.0 * math.pi / total)
    sine = jnp.sin(theta)[:, :, None, None]
    halfsq = (jnp.sin(0.5 * theta) ** 2)[:, :, None, None]
    parity = (1 - 2 * (freq % 2)).astype(jnp.float32)[:, :, None, None]
    shape_out = freq.shape + (pole.shape[0],)
    real_part = jnp.zeros(shape_out, jnp.float32)
    imag_part = jnp.zeros(shape_out, jnp.float32)
    for first in range(0, pole.shape[1], 4):
        part_pole = pole[:, first : first + 4]
        dreal = gap[:, first : first + 4] + 2.0 * part_pole * halfsq
        dimag = part_pole * sine
        factor = (
            scale[:, first : first + 4]
            * (1.0 - tail[:, first : first + 4] * parity)
            / (dreal * dreal + dimag * dimag)
        )
        real_part = real_part + jnp.sum(factor * dreal, axis=-1)
        imag_part = imag_part - jnp.sum(factor * dimag, axis=-1)
    return (real_part, imag_part)


def convolve(gated, skip, filters, total, move_forward, move_back):
    pieces, block, width = gated.shape
    span = 2 * pieces
    outer_index = jnp.arange(span, dtype=jnp.int32)
    piece_index = jnp.arange(pieces, dtype=jnp.int32)
    outer_cos, outer_sin = angle_tables(outer_index, piece_index, span)
    real_part = jnp.einsum("kp,ptc->ktc", outer_cos, gated, precision=HIGHEST)
    imag_part = -jnp.einsum("kp,ptc->ktc", outer_sin, gated, precision=HIGHEST)
    times = jnp.arange(block, dtype=jnp.int32)
    twist_cos, twist_sin = angle_tables(outer_index, times, total)
    twist_cos = twist_cos[:, :, None]
    twist_sin = twist_sin[:, :, None]
    turned_real = twist_cos * real_part + twist_sin * imag_part
    turned_imag = twist_cos * imag_part - twist_sin * real_part
    moved = move_forward(jnp.stack([turned_real, turned_imag]))
    count = moved.shape[1]
    length = moved.shape[2]
    positions = jnp.arange(length, dtype=jnp.int32)
    inner_cos, inner_sin = angle_tables(positions, positions, length)
    freq_real = jnp.einsum("mt,ktc->kmc", inner_cos, moved[0], precision=HIGHEST) + jnp.einsum(
        "mt,ktc->kmc", inner_sin, moved[1], precision=HIGHEST
    )
    freq_imag = jnp.einsum("mt,ktc->kmc", inner_cos, moved[1], precision=HIGHEST) - jnp.einsum(
        "mt,ktc->kmc", inner_sin, moved[0], precision=HIGHEST
    )
    owned = jnp.arange(count, dtype=jnp.int32)
    freq = (owned[:, None] + span * positions[None, :]) % total
    filt_real, filt_imag = filter_spectrum(freq, total, *filters)
    prod_real = freq_real * filt_real - freq_imag * filt_imag
    prod_imag = freq_real * filt_imag + freq_imag * filt_real
    back_real = jnp.einsum("mt,kmc->ktc", inner_cos, prod_real, precision=HIGHEST) - jnp.einsum(
        "mt,kmc->ktc", inner_sin, prod_imag, precision=HIGHEST
    )
    back_imag = jnp.einsum("mt,kmc->ktc", inner_cos, prod_imag, precision=HIGHEST) + jnp.einsum(
        "mt,kmc->ktc", inner_sin, prod_real, precision=HIGHEST
    )
    undo_cos, undo_sin = angle_tables(owned, positions, total)
    undo_cos = undo_cos[:, :, None]
    undo_sin = undo_sin[:, :, None]
    untwist_real = undo_cos * back_real - undo_sin * back_imag
    untwist_imag = undo_cos * back_imag + undo_sin * back_real
    returned = move_back(jnp.stack([untwist_real, untwist_imag]))
    last_cos, last_sin = angle_tables(piece_index, outer_index, span)
    convolved = (
        jnp.einsum("pk,ktc->ptc", last_cos, returned[0], precision=HIGHEST)
        - jnp.einsum("pk,ktc->ptc", last_sin, returned[1], precision=HIGHEST)
    ) * (1.0 / total)
    return convolved + skip * gated


def unchanged(value):
    return value


def body(token_ids, vocab_table, short_filter, residue, decay, skip_gain):
    pieces = lax.axis_size("seq")
    place = lax.axis_index("seq")
    length = token_ids.shape[0]
    local = length // pieces
    share = vocab_table.shape[2]
    rim = short_filter.shape[0] - 1
    total = 2 * length
    rate = decay / length
    pole = jnp.exp(-rate)
    gap = -jnp.expm1(-rate)
    tail = jnp.exp(-decay)
    scale = residue * jnp.sqrt(2.0 * rate)
    first_channel = place * share
    chan_taps = lax.dynamic_slice_in_dim(short_filter, first_channel, share, 2)
    chan_filters = (
        lax.dynamic_slice_in_dim(pole, first_channel, share, 0),
        lax.dynamic_slice_in_dim(gap, first_channel, share, 0),
        lax.dynamic_slice_in_dim(tail, first_channel, share, 0),
        lax.dynamic_slice_in_dim(scale, first_channel, share, 0),
    )
    chan_skip = lax.dynamic_slice_in_dim(skip_gain, first_channel, share, 0)
    entries = jnp.arange(vocab_table.shape[0], dtype=token_ids.dtype)
    chosen = (token_ids[:, None] == entries[None, :]).astype(vocab_table.dtype)
    streams = jnp.einsum("nv,vjc->njc", chosen, vocab_table, preferred_element_type=jnp.float32)
    padded = jnp.pad(streams, ((rim, 0), (0, 0), (0, 0)))
    mixed = short_conv(padded, chan_taps, length)
    query = mixed[:, 0]
    gated = (mixed[:, 1] * mixed[:, 2]).reshape(pieces, local, share)
    convolved = convolve(gated, chan_skip, chan_filters, total, unchanged, unchanged)
    output = (query * convolved.reshape(length, share)).astype(jnp.bfloat16)
    return lax.all_to_all(output, "seq", split_axis=0, concat_axis=1, tiled=True)


LANES = 128
SUB = 8
HALO = 8
UNROLL = 8
CUTS = 4
PARTS = 8
MESH = pl.DeviceIdType.MESH


def wide(row):
    return jnp.broadcast_to(row, (SUB, LANES))


def toggles(value, limit):
    steps, bit = [], 1
    while bit < limit:
        steps.append((bit, bit - 2 * bit * (value // bit % 2)))
        bit = 2 * bit
    return steps


def flip(value, steps, mask):
    for bit, step in steps:
        if mask & bit:
            value = value + step
    return value


def scan_kernel(
    pieces,
    local,
    width,
    modes,
    all_ids_ref,
    all_tab_ref,
    all_taps_ref,
    all_decay_ref,
    all_residue_ref,
    all_skip_ref,
    out_ref,
    ids_ref,
    tab_ref,
    taps_ref,
    decay_ref,
    residue_ref,
    skip_ref,
    load_sem,
    ids_sem,
    hot_ref,
    x_ref,
    query_ref,
    gated_ref,
    end_ref,
    begin_ref,
    carry_ref,
    coef_ref,
    turn_ref,
    send_ref,
    send_sem,
    recv_sem,
    own_sem,
):
    me = lax.axis_index("seq")
    half = me // SUB
    share = 2 * LANES
    vocab = tab_ref.shape[2]
    length = pieces * local
    steps = toggles(me, SUB)

    def loads(block):
        mine = pl.ds(pl.multiple_of(me * share + block * LANES, LANES), LANES)
        lane = pl.ds(block * LANES, LANES)
        pairs = (
            (all_tab_ref.at[:, :, lane], tab_ref.at[block]),
            (all_taps_ref.at[:, :, mine], taps_ref.at[block]),
            (all_decay_ref.at[:, mine], decay_ref.at[block]),
            (all_residue_ref.at[:, mine], residue_ref.at[block]),
            (all_skip_ref.at[:, mine], skip_ref.at[block]),
        )
        return [
            pltpu.make_async_copy(source, target, load_sem.at[block, i])
            for i, (source, target) in enumerate(pairs)
        ]

    load_ids = pltpu.make_async_copy(all_ids_ref, ids_ref, ids_sem.at[0])
    load_ids.start()
    for block in range(2):
        for load in loads(block):
            load.start()
    barrier = pltpu.get_barrier_semaphore()

    def greet(i, _):
        peer = me + i - pieces * ((me + i) // pieces)
        pl.semaphore_signal(barrier, inc=1, device_id={"seq": peer}, device_id_type=MESH)
        return 0

    lax.fori_loop(1, pieces, greet, 0)

    load_ids.wait()
    ids = ids_ref[...]
    before = jnp.where(
        lax.broadcasted_iota(jnp.int32, ids.shape, 0) == 0, -1, pltpu.roll(ids, 1, axis=0)
    )
    entry = lax.broadcasted_iota(jnp.int16, (2 * SUB, vocab), 1)

    count = (HALO + local) // CUTS
    one = jnp.ones(entry.shape, jnp.bfloat16)
    nought = jnp.zeros(entry.shape, jnp.bfloat16)

    def build(slot, i):
        rows = slice(slot * SUB, (slot + 1) * SUB)
        for t in range(i * count - HALO, (i + 1) * count - HALO, 2):
            pair = []
            for at in (t, t + 1):
                column = (
                    ids[rows, at : at + 1] if at >= 0 else before[rows, local + at : local + at + 1]
                )
                pair.append(jnp.broadcast_to(column, (SUB, LANES)))
            pair = jnp.concatenate(pair, axis=0).astype(jnp.int16)
            pair = jnp.concatenate([pair] * (vocab // LANES), axis=1)
            hot_ref[slot, (HALO + t) * SUB : (HALO + t + 2) * SUB, :] = jnp.where(
                pair == entry, one, nought
            )

    everything = pl.ds(0, local)

    def place(block, source, span):
        return out_ref.at[
            span, pl.ds(pl.multiple_of(source * share + block * LANES, LANES), LANES)
        ]

    def remote(block, slot, low, sender, span=everything):
        peer = slot * SUB + low
        return pltpu.make_async_remote_copy(
            src_ref=send_ref.at[block, peer, span],
            dst_ref=place(block, sender, span),
            send_sem=send_sem.at[block, peer],
            recv_sem=recv_sem.at[block, sender],
            device_id={"seq": peer},
            device_id_type=MESH,
        )

    def own(block, span=everything):
        return pltpu.make_async_copy(
            send_ref.at[block, me, span], place(block, me, span), own_sem.at[block]
        )

    cut = (HALO + local) * SUB // CUTS

    def taps_of(block, j):
        return [wide(taps_ref[block, j, lag : lag + 1, :]) for lag in range(width)]

    def mix(rows_ref, taps, i):
        seen = {}
        for t in range(1 - width, UNROLL):
            at = pl.multiple_of((i * UNROLL + t + HALO) * SUB, SUB)
            seen[t] = rows_ref[pl.ds(at, SUB), :]
        totals = []
        for t in range(UNROLL):
            total = taps[0] * seen[t]
            for lag in range(1, width):
                total = total + taps[lag] * seen[t - lag]
            totals.append(total)
        return totals

    def head(block, slot):
        if block == 0:
            build(slot, 0)
        if slot == 0:
            for load in loads(block):
                load.wait()
            rate = decay_ref[block] / length
            coef_ref[0] = jnp.exp(-rate)
            coef_ref[1] = residue_ref[block] * jnp.sqrt(2.0 * rate)
            coef_ref[2] = jnp.exp(-rate * local)
            carry_ref[...] = jnp.zeros_like(carry_ref)

        table = jnp.concatenate([tab_ref[block, j] for j in (1, 2)], axis=1)
        for i in range(CUTS):
            if block == 0 and i + 1 < CUTS:
                build(slot, i + 1)
            span = pl.ds(i * cut, cut)
            x_ref[span, :] = jnp.dot(
                hot_ref[slot, span, :], table, preferred_element_type=jnp.float32
            )
        poles = [wide(coef_ref[0, s : s + 1, :]) for s in range(modes)]
        taps = [taps_of(block, j) for j in (1, 2)]

        def step(i, state):
            state = list(state)
            mixed = [
                mix(x_ref.at[:, j * LANES : (j + 1) * LANES], taps[j], i) for j in range(2)
            ]
            for t in range(UNROLL):
                at = pl.multiple_of((i * UNROLL + t) * SUB, SUB)
                gated = mixed[0][t] * mixed[1][t]
                gated_ref[slot, pl.ds(at, SUB), :] = gated
                for s in range(modes):
                    state[s] = poles[s] * state[s] + gated
            return tuple(state)

        zero = jnp.zeros((SUB, LANES), jnp.float32)
        state = lax.fori_loop(0, local // UNROLL, step, (zero,) * modes)
        for s in range(modes):
            end_ref[s * SUB : (s + 1) * SUB, :] = state[s]
        leap = coef_ref[2]
        carry = carry_ref[...]
        for k in range(SUB):
            begin_ref[slot, pl.ds(k, modes, stride=SUB), :] = carry
            carry = leap * carry + end_ref[pl.ds(k, modes, stride=SUB), :]
        carry_ref[...] = carry

    def tail(block, slot, first):
        poles = [wide(coef_ref[0, s : s + 1, :]) for s in range(modes)]
        coefs = [wide(coef_ref[1, s : s + 1, :]) for s in range(modes)]
        skip = wide(skip_ref[block])
        taps = taps_of(block, 0)
        query_ref[...] = jnp.dot(
            hot_ref[slot], tab_ref[block, 0], preferred_element_type=jnp.float32
        )

        def step(i, state):
            state = list(state)
            query = mix(query_ref, taps, i)
            for t in range(UNROLL):
                at = pl.multiple_of((i * UNROLL + t) * SUB, SUB)
                gated = gated_ref[slot, pl.ds(at, SUB), :]
                terms = [skip * gated]
                for s in range(modes):
                    state[s] = poles[s] * state[s] + gated
                    terms.append(coefs[s] * state[s])
                    if len(terms) == 5:
                        terms = [((terms[0] + terms[1]) + (terms[2] + terms[3])) + terms[4]]
                total = terms[0]
                for term in terms[1:]:
                    total = total + term
                turn_ref[pl.ds(at, SUB), :] = query[t] * total
            return tuple(state)

        state = tuple(begin_ref[slot, s * SUB : (s + 1) * SUB, :] for s in range(modes))
        parts = PARTS if block == 0 else 1
        height = local // parts
        for part in range(parts):
            span = pl.ds(part * height, height)
            state = lax.fori_loop(
                part * height // UNROLL, (part + 1) * height // UNROLL, step, state
            )
            for k in range(SUB):
                send_ref[block, slot * SUB + k, span, :] = turn_ref[
                    pl.ds(part * height * SUB + k, height, stride=SUB), :
                ].astype(jnp.bfloat16)

            if part == 0:

                @pl.when(first)
                def _():
                    pl.semaphore_wait(barrier, pieces - 1)

            for low in range(SUB):

                @pl.when(slot * SUB + low != me)
                def _():
                    remote(block, slot, low, me, span).start()

            @pl.when(slot == half)
            def _():
                own(block, span).start()

    for block in range(2):
        head(block, 0)

        def early(i, _):
            tail(block, 0, block == 0)
            return 0

        lax.fori_loop(0, half, early, 0)
        head(block, 1)

        def late(i, _):
            tail(block, 1 - i, jnp.logical_and(half + i == 0, block == 0))
            return 0

        lax.fori_loop(0, 2 - half, late, 0)

    for block in range(2):
        own(block).wait()

        def finish(i, _):
            peer = me + i - pieces * ((me + i) // pieces)
            remote(block, peer // SUB, peer - peer // SUB * SUB, me).wait_send()
            remote(block, half, me - half * SUB, peer).wait_recv()
            return 0

        lax.fori_loop(1, pieces, finish, 0)


def scan_body(token_ids, vocab_table, short_filter, residue, decay, skip_gain):
    pieces = lax.axis_size("seq")
    length = token_ids.shape[0]
    local = length // pieces
    vocab, streams, share = vocab_table.shape
    width = short_filter.shape[0]
    modes = decay.shape[1]
    ids = token_ids.reshape(pieces, local)
    table = vocab_table.transpose(1, 0, 2)
    taps = short_filter.transpose(1, 0, 2)
    rows = (HALO + local) * SUB
    return pl.pallas_call(
        functools.partial(scan_kernel, pieces, local, width, modes),
        out_shape=pltpu.VMEM((local, pieces * share), jnp.bfloat16),
        in_specs=[pl.BlockSpec(memory_space=pl.ANY)] * 6,
        out_specs=pl.BlockSpec(memory_space=pltpu.VMEM),
        scratch_shapes=[
            pltpu.VMEM((pieces, local), jnp.int32),
            pltpu.VMEM((2, streams, vocab, LANES), vocab_table.dtype),
            pltpu.VMEM((2, streams, width, LANES), jnp.float32),
            pltpu.VMEM((2, modes, LANES), jnp.float32),
            pltpu.VMEM((2, modes, LANES), jnp.float32),
            pltpu.VMEM((2, 1, LANES), jnp.float32),
            pltpu.SemaphoreType.DMA((2, 5)),
            pltpu.SemaphoreType.DMA((1,)),
            pltpu.VMEM((2, rows, vocab), jnp.bfloat16),
            pltpu.VMEM((rows, 2 * LANES), jnp.float32),
            pltpu.VMEM((rows, LANES), jnp.float32),
            pltpu.VMEM((2, local * SUB, LANES), jnp.float32),
            pltpu.VMEM((modes * SUB, LANES), jnp.float32),
            pltpu.VMEM((2, modes * SUB, LANES), jnp.float32),
            pltpu.VMEM((modes, LANES), jnp.float32),
            pltpu.VMEM((3, modes, LANES), jnp.float32),
            pltpu.VMEM((local * SUB, LANES), jnp.float32),
            pltpu.VMEM((2, pieces, local, LANES), jnp.bfloat16),
            pltpu.SemaphoreType.DMA((2, pieces)),
            pltpu.SemaphoreType.DMA((2, pieces)),
            pltpu.SemaphoreType.DMA((2,)),
        ],
        compiler_params=pltpu.CompilerParams(collective_id=0, has_side_effects=True),
    )(ids, table, taps, decay.T, residue.T, skip_gain[None])


def fits(mesh, share, local, width, streams):
    even = mesh.shape["seq"] == 2 * SUB
    return even and share == 2 * LANES and local == LANES and width <= HALO + 1 and streams == 3


def solution(mesh):
    placed = (P("groups"), P(None, None, "seq"), P(), P(), P(), P())

    def whole(token_ids, vocab_table, short_filter, residue, decay, skip_gain):
        pieces = mesh.shape["seq"]
        local = token_ids.shape[0] // (mesh.shape["groups"] * pieces)
        share = vocab_table.shape[2] // pieces
        shapes = (share, local, short_filter.shape[0], vocab_table.shape[1])
        chosen = scan_body if fits(mesh, *shapes) else body
        return jax.shard_map(
            chosen, mesh=mesh, in_specs=placed, out_specs=P(("groups", "seq"), None), check_vma=False
        )(token_ids, vocab_table, short_filter, residue, decay, skip_gain)

    return whole
```

```python
import functools
import math

import jax
import jax.numpy as jnp
from jax import lax
from jax.experimental import pallas as pl
from jax.experimental.pallas import tpu as pltpu
from jax.sharding import PartitionSpec as P

HIGHEST = lax.Precision.HIGHEST


def angle_tables(first_index, second_index, modulus):
    product = first_index[:, None] * second_index[None, :] % modulus
    angle = product.astype(jnp.float32) * (2.0 * math.pi / modulus)
    return (jnp.cos(angle), jnp.sin(angle))


def short_conv(padded, taps, count):
    width = taps.shape[0]
    total = jnp.zeros((count,) + padded.shape[1:], jnp.float32)
    for lag in range(width):
        start = width - 1 - lag
        total = total + taps[lag] * padded[start : start + count].astype(jnp.float32)
    return total


def filter_spectrum(freq, total, pole, gap, tail, scale):
    theta = freq.astype(jnp.float32) * (2.0 * math.pi / total)
    sine = jnp.sin(theta)[:, :, None, None]
    halfsq = (jnp.sin(0.5 * theta) ** 2)[:, :, None, None]
    parity = (1 - 2 * (freq % 2)).astype(jnp.float32)[:, :, None, None]
    shape_out = freq.shape + (pole.shape[0],)
    real_part = jnp.zeros(shape_out, jnp.float32)
    imag_part = jnp.zeros(shape_out, jnp.float32)
    for first in range(0, pole.shape[1], 4):
        part_pole = pole[:, first : first + 4]
        dreal = gap[:, first : first + 4] + 2.0 * part_pole * halfsq
        dimag = part_pole * sine
        factor = (
            scale[:, first : first + 4]
            * (1.0 - tail[:, first : first + 4] * parity)
            / (dreal * dreal + dimag * dimag)
        )
        real_part = real_part + jnp.sum(factor * dreal, axis=-1)
        imag_part = imag_part - jnp.sum(factor * dimag, axis=-1)
    return (real_part, imag_part)


def convolve(gated, skip, filters, total, move_forward, move_back):
    pieces, block, width = gated.shape
    span = 2 * pieces
    outer_index = jnp.arange(span, dtype=jnp.int32)
    piece_index = jnp.arange(pieces, dtype=jnp.int32)
    outer_cos, outer_sin = angle_tables(outer_index, piece_index, span)
    real_part = jnp.einsum("kp,ptc->ktc", outer_cos, gated, precision=HIGHEST)
    imag_part = -jnp.einsum("kp,ptc->ktc", outer_sin, gated, precision=HIGHEST)
    times = jnp.arange(block, dtype=jnp.int32)
    twist_cos, twist_sin = angle_tables(outer_index, times, total)
    twist_cos = twist_cos[:, :, None]
    twist_sin = twist_sin[:, :, None]
    turned_real = twist_cos * real_part + twist_sin * imag_part
    turned_imag = twist_cos * imag_part - twist_sin * real_part
    moved = move_forward(jnp.stack([turned_real, turned_imag]))
    count = moved.shape[1]
    length = moved.shape[2]
    positions = jnp.arange(length, dtype=jnp.int32)
    inner_cos, inner_sin = angle_tables(positions, positions, length)
    freq_real = jnp.einsum("mt,ktc->kmc", inner_cos, moved[0], precision=HIGHEST) + jnp.einsum(
        "mt,ktc->kmc", inner_sin, moved[1], precision=HIGHEST
    )
    freq_imag = jnp.einsum("mt,ktc->kmc", inner_cos, moved[1], precision=HIGHEST) - jnp.einsum(
        "mt,ktc->kmc", inner_sin, moved[0], precision=HIGHEST
    )
    owned = jnp.arange(count, dtype=jnp.int32)
    freq = (owned[:, None] + span * positions[None, :]) % total
    filt_real, filt_imag = filter_spectrum(freq, total, *filters)
    prod_real = freq_real * filt_real - freq_imag * filt_imag
    prod_imag = freq_real * filt_imag + freq_imag * filt_real
    back_real = jnp.einsum("mt,kmc->ktc", inner_cos, prod_real, precision=HIGHEST) - jnp.einsum(
        "mt,kmc->ktc", inner_sin, prod_imag, precision=HIGHEST
    )
    back_imag = jnp.einsum("mt,kmc->ktc", inner_cos, prod_imag, precision=HIGHEST) + jnp.einsum(
        "mt,kmc->ktc", inner_sin, prod_real, precision=HIGHEST
    )
    undo_cos, undo_sin = angle_tables(owned, positions, total)
    undo_cos = undo_cos[:, :, None]
    undo_sin = undo_sin[:, :, None]
    untwist_real = undo_cos * back_real - undo_sin * back_imag
    untwist_imag = undo_cos * back_imag + undo_sin * back_real
    returned = move_back(jnp.stack([untwist_real, untwist_imag]))
    last_cos, last_sin = angle_tables(piece_index, outer_index, span)
    convolved = (
        jnp.einsum("pk,ktc->ptc", last_cos, returned[0], precision=HIGHEST)
        - jnp.einsum("pk,ktc->ptc", last_sin, returned[1], precision=HIGHEST)
    ) * (1.0 / total)
    return convolved + skip * gated


def unchanged(value):
    return value


def body(token_ids, vocab_table, short_filter, residue, decay, skip_gain):
    pieces = lax.axis_size("seq")
    place = lax.axis_index("seq")
    length = token_ids.shape[0]
    local = length // pieces
    share = vocab_table.shape[2]
    rim = short_filter.shape[0] - 1
    total = 2 * length
    rate = decay / length
    pole = jnp.exp(-rate)
    gap = -jnp.expm1(-rate)
    tail = jnp.exp(-decay)
    scale = residue * jnp.sqrt(2.0 * rate)
    first_channel = place * share
    chan_taps = lax.dynamic_slice_in_dim(short_filter, first_channel, share, 2)
    chan_filters = (
        lax.dynamic_slice_in_dim(pole, first_channel, share, 0),
        lax.dynamic_slice_in_dim(gap, first_channel, share, 0),
        lax.dynamic_slice_in_dim(tail, first_channel, share, 0),
        lax.dynamic_slice_in_dim(scale, first_channel, share, 0),
    )
    chan_skip = lax.dynamic_slice_in_dim(skip_gain, first_channel, share, 0)
    entries = jnp.arange(vocab_table.shape[0], dtype=token_ids.dtype)
    chosen = (token_ids[:, None] == entries[None, :]).astype(vocab_table.dtype)
    streams = jnp.einsum("nv,vjc->njc", chosen, vocab_table, preferred_element_type=jnp.float32)
    padded = jnp.pad(streams, ((rim, 0), (0, 0), (0, 0)))
    mixed = short_conv(padded, chan_taps, length)
    query = mixed[:, 0]
    gated = (mixed[:, 1] * mixed[:, 2]).reshape(pieces, local, share)
    convolved = convolve(gated, chan_skip, chan_filters, total, unchanged, unchanged)
    output = (query * convolved.reshape(length, share)).astype(jnp.bfloat16)
    return lax.all_to_all(output, "seq", split_axis=0, concat_axis=1, tiled=True)


LANES = 128
SUB = 8
HALO = 8
LONG = 32
UNROLL = 16
CUTS = 4
FAR = (16, 32, 80,)
MESH = pl.DeviceIdType.MESH


def wide(row):
    return jnp.broadcast_to(row, (SUB, LANES))


def toggles(value, limit):
    steps, bit = [], 1
    while bit < limit:
        steps.append((bit, bit - 2 * bit * (value // bit % 2)))
        bit = 2 * bit
    return steps


def flip(value, steps, mask):
    for bit, step in steps:
        if mask & bit:
            value = value + step
    return value


def scan_kernel(
    pieces,
    local,
    width,
    modes,
    all_ids_ref,
    all_tab_ref,
    all_taps_ref,
    all_decay_ref,
    all_residue_ref,
    all_skip_ref,
    out_ref,
    ids_ref,
    tab_ref,
    taps_ref,
    decay_ref,
    residue_ref,
    skip_ref,
    load_sem,
    ids_sem,
    hot_ref,
    x_ref,
    query_ref,
    gated_ref,
    end_ref,
    begin_ref,
    carry_ref,
    coef_ref,
    turn_ref,
    send_ref,
    send_sem,
    recv_sem,
    own_sem,
):
    me = lax.axis_index("seq")
    half = me // SUB
    share = 2 * LANES
    vocab = tab_ref.shape[2]
    length = pieces * local
    steps = toggles(me, SUB)

    def loads(block):
        mine = pl.ds(pl.multiple_of(me * share + block * LANES, LANES), LANES)
        lane = pl.ds(block * LANES, LANES)
        pairs = (
            (all_tab_ref.at[:, :, lane], tab_ref.at[block]),
            (all_taps_ref.at[:, :, mine], taps_ref.at[block]),
            (all_decay_ref.at[:, mine], decay_ref.at[block]),
            (all_residue_ref.at[:, mine], residue_ref.at[block]),
            (all_skip_ref.at[:, mine], skip_ref.at[block]),
        )
        return [
            pltpu.make_async_copy(source, target, load_sem.at[block, i])
            for i, (source, target) in enumerate(pairs)
        ]

    load_ids = pltpu.make_async_copy(all_ids_ref, ids_ref, ids_sem.at[0])
    load_ids.start()
    for block in range(2):
        for load in loads(block):
            load.start()
    barrier = pltpu.get_barrier_semaphore()

    def greet(i, _):
        peer = me + i - pieces * ((me + i) // pieces)
        pl.semaphore_signal(barrier, inc=1, device_id={"seq": peer}, device_id_type=MESH)
        return 0

    lax.fori_loop(1, pieces, greet, 0)

    load_ids.wait()
    ids = ids_ref[...]
    before = jnp.where(
        lax.broadcasted_iota(jnp.int32, ids.shape, 0) == 0, -1, pltpu.roll(ids, 1, axis=0)
    )
    entry = lax.broadcasted_iota(jnp.int16, (2 * SUB, vocab), 1)

    count = (HALO + local) // CUTS
    one = jnp.ones(entry.shape, jnp.bfloat16)
    nought = jnp.zeros(entry.shape, jnp.bfloat16)

    def build(slot, i):
        rows = slice(slot * SUB, (slot + 1) * SUB)
        for t in range(i * count - HALO, (i + 1) * count - HALO, 2):
            pair = []
            for at in (t, t + 1):
                column = (
                    ids[rows, at : at + 1] if at >= 0 else before[rows, local + at : local + at + 1]
                )
                pair.append(jnp.broadcast_to(column, (SUB, LANES)))
            pair = jnp.concatenate(pair, axis=0).astype(jnp.int16)
            pair = jnp.concatenate([pair] * (vocab // LANES), axis=1)
            hot_ref[slot, (HALO + t) * SUB : (HALO + t + 2) * SUB, :] = jnp.where(
                pair == entry, one, nought
            )

    everything = pl.ds(0, local)

    def place(block, source, span):
        return out_ref.at[
            span, pl.ds(pl.multiple_of(source * share + block * LANES, LANES), LANES)
        ]

    def remote(block, slot, low, sender, span=everything):
        peer = slot * SUB + low
        return pltpu.make_async_remote_copy(
            src_ref=send_ref.at[block, peer, span],
            dst_ref=place(block, sender, span),
            send_sem=send_sem.at[block, peer],
            recv_sem=recv_sem.at[block, sender],
            device_id={"seq": peer},
            device_id_type=MESH,
        )

    def own(block, span=everything):
        return pltpu.make_async_copy(
            send_ref.at[block, me, span], place(block, me, span), own_sem.at[block]
        )

    cut = (HALO + local) * SUB // CUTS

    def taps_of(block, j):
        return [wide(taps_ref[block, j, lag : lag + 1, :]) for lag in range(width)]

    def mix(rows_ref, taps, i, unroll):
        seen = {}
        for t in range(1 - width, unroll):
            at = pl.multiple_of((i * unroll + t + HALO) * SUB, SUB)
            seen[t] = rows_ref[pl.ds(at, SUB), :]
        totals = []
        for t in range(unroll):
            total = taps[0] * seen[t]
            for lag in range(1, width):
                total = total + taps[lag] * seen[t - lag]
            totals.append(total)
        return totals

    def head(block, slot):
        if block == 0:
            build(slot, 0)
        if slot == 0:
            for load in loads(block):
                load.wait()
            rate = decay_ref[block] / length
            coef_ref[0] = jnp.exp(-rate)
            coef_ref[1] = residue_ref[block] * jnp.sqrt(2.0 * rate)
            coef_ref[2] = jnp.exp(-rate * local)
            carry_ref[...] = jnp.zeros_like(carry_ref)

        table = jnp.concatenate([tab_ref[block, j] for j in (1, 2)], axis=1)
        for i in range(CUTS):
            if block == 0 and i + 1 < CUTS:
                build(slot, i + 1)
            span = pl.ds(i * cut, cut)
            x_ref[span, :] = jnp.dot(
                hot_ref[slot, span, :], table, preferred_element_type=jnp.float32
            )
        poles = [wide(coef_ref[0, s : s + 1, :]) for s in range(modes)]
        taps = [taps_of(block, j) for j in (1, 2)]

        def step(i, state):
            state = list(state)
            mixed = [
                mix(x_ref.at[:, j * LANES : (j + 1) * LANES], taps[j], i, LONG) for j in range(2)
            ]
            for t in range(LONG):
                at = pl.multiple_of((i * LONG + t) * SUB, SUB)
                gated = mixed[0][t] * mixed[1][t]
                gated_ref[slot, pl.ds(at, SUB), :] = gated
                for s in range(modes):
                    state[s] = poles[s] * state[s] + gated
            return tuple(state)

        zero = jnp.zeros((SUB, LANES), jnp.float32)
        state = lax.fori_loop(0, local // LONG, step, (zero,) * modes)
        for s in range(modes):
            end_ref[s * SUB : (s + 1) * SUB, :] = state[s]
        leap = coef_ref[2]
        carry = carry_ref[...]
        for k in range(SUB):
            begin_ref[slot, pl.ds(k, modes, stride=SUB), :] = carry
            carry = leap * carry + end_ref[pl.ds(k, modes, stride=SUB), :]
        carry_ref[...] = carry

    def tail(block, slot, first, heights):
        poles = [wide(coef_ref[0, s : s + 1, :]) for s in range(modes)]
        coefs = [wide(coef_ref[1, s : s + 1, :]) for s in range(modes)]
        skip = wide(skip_ref[block])
        taps = taps_of(block, 0)
        query_ref[...] = jnp.dot(
            hot_ref[slot], tab_ref[block, 0], preferred_element_type=jnp.float32
        )

        def step(i, state):
            state = list(state)
            query = mix(query_ref, taps, i, UNROLL)
            for t in range(UNROLL):
                at = pl.multiple_of((i * UNROLL + t) * SUB, SUB)
                gated = gated_ref[slot, pl.ds(at, SUB), :]
                terms = [skip * gated]
                for s in range(modes):
                    state[s] = poles[s] * state[s] + gated
                    terms.append(coefs[s] * state[s])
                    if len(terms) == 5:
                        terms = [((terms[0] + terms[1]) + (terms[2] + terms[3])) + terms[4]]
                total = terms[0]
                for term in terms[1:]:
                    total = total + term
                turn_ref[pl.ds(at, SUB), :] = query[t] * total
            return tuple(state)

        state = tuple(begin_ref[slot, s * SUB : (s + 1) * SUB, :] for s in range(modes))
        low_end = 0
        for part, height in enumerate(heights):
            start, low_end = low_end, low_end + height
            span = pl.ds(start, height)
            state = lax.fori_loop(start // UNROLL, low_end // UNROLL, step, state)
            for k in range(SUB):
                send_ref[block, slot * SUB + k, span, :] = turn_ref[
                    pl.ds(start * SUB + k, height, stride=SUB), :
                ].astype(jnp.bfloat16)

            if first and part == 0:
                pl.semaphore_wait(barrier, pieces - 1)

            for low in range(SUB):

                @pl.when(slot * SUB + low != me)
                def _():
                    remote(block, slot, low, me, span).start()

            @pl.when(slot == half)
            def _():
                own(block, span).start()

    for block in range(2):
        head(block, 0)
        far = FAR if block == 0 else (local,)

        def early(i, _):
            tail(block, 0, block == 0, far)
            return 0

        lax.fori_loop(0, half, early, 0)
        head(block, 1)

        def far_late(i, _):
            tail(block, 1, block == 0, far)
            return 0

        lax.fori_loop(0, 1 - half, far_late, 0)

        def near_late(i, _):
            tail(block, half, False, (local,))
            return 0

        lax.fori_loop(0, 1, near_late, 0)

    for block in range(2):
        own(block).wait()

        def finish(i, _):
            peer = me + i - pieces * ((me + i) // pieces)
            remote(block, peer // SUB, peer - peer // SUB * SUB, me).wait_send()
            remote(block, half, me - half * SUB, peer).wait_recv()
            return 0

        lax.fori_loop(1, pieces, finish, 0)


def scan_body(token_ids, vocab_table, short_filter, residue, decay, skip_gain):
    pieces = lax.axis_size("seq")
    length = token_ids.shape[0]
    local = length // pieces
    vocab, streams, share = vocab_table.shape
    width = short_filter.shape[0]
    modes = decay.shape[1]
    ids = token_ids.reshape(pieces, local)
    table = vocab_table.transpose(1, 0, 2)
    taps = short_filter.transpose(1, 0, 2)
    rows = (HALO + local) * SUB
    return pl.pallas_call(
        functools.partial(scan_kernel, pieces, local, width, modes),
        out_shape=pltpu.VMEM((local, pieces * share), jnp.bfloat16),
        in_specs=[pl.BlockSpec(memory_space=pl.ANY)] * 6,
        out_specs=pl.BlockSpec(memory_space=pltpu.VMEM),
        scratch_shapes=[
            pltpu.VMEM((pieces, local), jnp.int32),
            pltpu.VMEM((2, streams, vocab, LANES), vocab_table.dtype),
            pltpu.VMEM((2, streams, width, LANES), jnp.float32),
            pltpu.VMEM((2, modes, LANES), jnp.float32),
            pltpu.VMEM((2, modes, LANES), jnp.float32),
            pltpu.VMEM((2, 1, LANES), jnp.float32),
            pltpu.SemaphoreType.DMA((2, 5)),
            pltpu.SemaphoreType.DMA((1,)),
            pltpu.VMEM((2, rows, vocab), jnp.bfloat16),
            pltpu.VMEM((rows, 2 * LANES), jnp.float32),
            pltpu.VMEM((rows, LANES), jnp.float32),
            pltpu.VMEM((2, local * SUB, LANES), jnp.float32),
            pltpu.VMEM((modes * SUB, LANES), jnp.float32),
            pltpu.VMEM((2, modes * SUB, LANES), jnp.float32),
            pltpu.VMEM((modes, LANES), jnp.float32),
            pltpu.VMEM((3, modes, LANES), jnp.float32),
            pltpu.VMEM((local * SUB, LANES), jnp.float32),
            pltpu.VMEM((2, pieces, local, LANES), jnp.bfloat16),
            pltpu.SemaphoreType.DMA((2, pieces)),
            pltpu.SemaphoreType.DMA((2, pieces)),
            pltpu.SemaphoreType.DMA((2,)),
        ],
        compiler_params=pltpu.CompilerParams(collective_id=0, has_side_effects=True),
    )(ids, table, taps, decay.T, residue.T, skip_gain[None])


def fits(mesh, share, local, width, streams):
    even = mesh.shape["seq"] == 2 * SUB
    return even and share == 2 * LANES and local == LANES and width <= HALO + 1 and streams == 3


def solution(mesh):
    placed = (P("groups"), P(None, None, "seq"), P(), P(), P(), P())

    def whole(token_ids, vocab_table, short_filter, residue, decay, skip_gain):
        pieces = mesh.shape["seq"]
        local = token_ids.shape[0] // (mesh.shape["groups"] * pieces)
        share = vocab_table.shape[2] // pieces
        shapes = (share, local, short_filter.shape[0], vocab_table.shape[1])
        chosen = scan_body if fits(mesh, *shapes) else body
        return jax.shard_map(
            chosen, mesh=mesh, in_specs=placed, out_specs=P(("groups", "seq"), None), check_vma=False
        )(token_ids, vocab_table, short_filter, residue, decay, skip_gain)

    return whole
```

```python
import functools
import math

import jax
import jax.numpy as jnp
from jax import lax
from jax.experimental import pallas as pl
from jax.experimental.pallas import tpu as pltpu
from jax.sharding import PartitionSpec as P

HIGHEST = lax.Precision.HIGHEST


def angle_tables(first_index, second_index, modulus):
    product = first_index[:, None] * second_index[None, :] % modulus
    angle = product.astype(jnp.float32) * (2.0 * math.pi / modulus)
    return (jnp.cos(angle), jnp.sin(angle))


def short_conv(padded, taps, count):
    width = taps.shape[0]
    total = jnp.zeros((count,) + padded.shape[1:], jnp.float32)
    for lag in range(width):
        start = width - 1 - lag
        total = total + taps[lag] * padded[start : start + count].astype(jnp.float32)
    return total


def filter_spectrum(freq, total, pole, gap, tail, scale):
    theta = freq.astype(jnp.float32) * (2.0 * math.pi / total)
    sine = jnp.sin(theta)[:, :, None, None]
    halfsq = (jnp.sin(0.5 * theta) ** 2)[:, :, None, None]
    parity = (1 - 2 * (freq % 2)).astype(jnp.float32)[:, :, None, None]
    shape_out = freq.shape + (pole.shape[0],)
    real_part = jnp.zeros(shape_out, jnp.float32)
    imag_part = jnp.zeros(shape_out, jnp.float32)
    for first in range(0, pole.shape[1], 4):
        part_pole = pole[:, first : first + 4]
        dreal = gap[:, first : first + 4] + 2.0 * part_pole * halfsq
        dimag = part_pole * sine
        factor = (
            scale[:, first : first + 4]
            * (1.0 - tail[:, first : first + 4] * parity)
            / (dreal * dreal + dimag * dimag)
        )
        real_part = real_part + jnp.sum(factor * dreal, axis=-1)
        imag_part = imag_part - jnp.sum(factor * dimag, axis=-1)
    return (real_part, imag_part)


def convolve(gated, skip, filters, total, move_forward, move_back):
    pieces, block, width = gated.shape
    span = 2 * pieces
    outer_index = jnp.arange(span, dtype=jnp.int32)
    piece_index = jnp.arange(pieces, dtype=jnp.int32)
    outer_cos, outer_sin = angle_tables(outer_index, piece_index, span)
    real_part = jnp.einsum("kp,ptc->ktc", outer_cos, gated, precision=HIGHEST)
    imag_part = -jnp.einsum("kp,ptc->ktc", outer_sin, gated, precision=HIGHEST)
    times = jnp.arange(block, dtype=jnp.int32)
    twist_cos, twist_sin = angle_tables(outer_index, times, total)
    twist_cos = twist_cos[:, :, None]
    twist_sin = twist_sin[:, :, None]
    turned_real = twist_cos * real_part + twist_sin * imag_part
    turned_imag = twist_cos * imag_part - twist_sin * real_part
    moved = move_forward(jnp.stack([turned_real, turned_imag]))
    count = moved.shape[1]
    length = moved.shape[2]
    positions = jnp.arange(length, dtype=jnp.int32)
    inner_cos, inner_sin = angle_tables(positions, positions, length)
    freq_real = jnp.einsum("mt,ktc->kmc", inner_cos, moved[0], precision=HIGHEST) + jnp.einsum(
        "mt,ktc->kmc", inner_sin, moved[1], precision=HIGHEST
    )
    freq_imag = jnp.einsum("mt,ktc->kmc", inner_cos, moved[1], precision=HIGHEST) - jnp.einsum(
        "mt,ktc->kmc", inner_sin, moved[0], precision=HIGHEST
    )
    owned = jnp.arange(count, dtype=jnp.int32)
    freq = (owned[:, None] + span * positions[None, :]) % total
    filt_real, filt_imag = filter_spectrum(freq, total, *filters)
    prod_real = freq_real * filt_real - freq_imag * filt_imag
    prod_imag = freq_real * filt_imag + freq_imag * filt_real
    back_real = jnp.einsum("mt,kmc->ktc", inner_cos, prod_real, precision=HIGHEST) - jnp.einsum(
        "mt,kmc->ktc", inner_sin, prod_imag, precision=HIGHEST
    )
    back_imag = jnp.einsum("mt,kmc->ktc", inner_cos, prod_imag, precision=HIGHEST) + jnp.einsum(
        "mt,kmc->ktc", inner_sin, prod_real, precision=HIGHEST
    )
    undo_cos, undo_sin = angle_tables(owned, positions, total)
    undo_cos = undo_cos[:, :, None]
    undo_sin = undo_sin[:, :, None]
    untwist_real = undo_cos * back_real - undo_sin * back_imag
    untwist_imag = undo_cos * back_imag + undo_sin * back_real
    returned = move_back(jnp.stack([untwist_real, untwist_imag]))
    last_cos, last_sin = angle_tables(piece_index, outer_index, span)
    convolved = (
        jnp.einsum("pk,ktc->ptc", last_cos, returned[0], precision=HIGHEST)
        - jnp.einsum("pk,ktc->ptc", last_sin, returned[1], precision=HIGHEST)
    ) * (1.0 / total)
    return convolved + skip * gated


def unchanged(value):
    return value


def body(token_ids, vocab_table, short_filter, residue, decay, skip_gain):
    pieces = lax.axis_size("seq")
    place = lax.axis_index("seq")
    length = token_ids.shape[0]
    local = length // pieces
    share = vocab_table.shape[2]
    rim = short_filter.shape[0] - 1
    total = 2 * length
    rate = decay / length
    pole = jnp.exp(-rate)
    gap = -jnp.expm1(-rate)
    tail = jnp.exp(-decay)
    scale = residue * jnp.sqrt(2.0 * rate)
    first_channel = place * share
    chan_taps = lax.dynamic_slice_in_dim(short_filter, first_channel, share, 2)
    chan_filters = (
        lax.dynamic_slice_in_dim(pole, first_channel, share, 0),
        lax.dynamic_slice_in_dim(gap, first_channel, share, 0),
        lax.dynamic_slice_in_dim(tail, first_channel, share, 0),
        lax.dynamic_slice_in_dim(scale, first_channel, share, 0),
    )
    chan_skip = lax.dynamic_slice_in_dim(skip_gain, first_channel, share, 0)
    entries = jnp.arange(vocab_table.shape[0], dtype=token_ids.dtype)
    chosen = (token_ids[:, None] == entries[None, :]).astype(vocab_table.dtype)
    streams = jnp.einsum("nv,vjc->njc", chosen, vocab_table, preferred_element_type=jnp.float32)
    padded = jnp.pad(streams, ((rim, 0), (0, 0), (0, 0)))
    mixed = short_conv(padded, chan_taps, length)
    query = mixed[:, 0]
    gated = (mixed[:, 1] * mixed[:, 2]).reshape(pieces, local, share)
    convolved = convolve(gated, chan_skip, chan_filters, total, unchanged, unchanged)
    output = (query * convolved.reshape(length, share)).astype(jnp.bfloat16)
    return lax.all_to_all(output, "seq", split_axis=0, concat_axis=1, tiled=True)


LANES = 128
SUB = 8
HALO = 8
LONG = 32
FIRST = (0, 1, 2, 3, 4, 5, 6, 7)
SECOND = (0, 4, 1, 5, 2, 6, 3, 7)
UNROLL = 16
CUTS = 4
FAR = (16, 32, 80,)
MESH = pl.DeviceIdType.MESH


def wide(row):
    return jnp.broadcast_to(row, (SUB, LANES))


def scan_kernel(
    pieces,
    local,
    width,
    modes,
    all_ids_ref,
    all_tab_ref,
    all_taps_ref,
    all_decay_ref,
    all_residue_ref,
    all_skip_ref,
    out_ref,
    ids_ref,
    tab_ref,
    taps_ref,
    decay_ref,
    residue_ref,
    skip_ref,
    load_sem,
    ids_sem,
    hot_ref,
    x_ref,
    query_ref,
    gated_ref,
    end_ref,
    begin_ref,
    carry_ref,
    coef_ref,
    turn_ref,
    send_ref,
    send_sem,
    recv_sem,
    own_sem,
):
    me = lax.axis_index("seq")
    half = me // SUB
    share = 2 * LANES
    vocab = tab_ref.shape[2]
    length = pieces * local

    def loads(block, picked=range(7)):
        mine = pl.ds(pl.multiple_of(me * share + block * LANES, LANES), LANES)
        lane = pl.ds(block * LANES, LANES)
        pairs = (
            (all_tab_ref.at[1, :, lane], tab_ref.at[block, 1]),
            (all_tab_ref.at[2, :, lane], tab_ref.at[block, 2]),
            (all_taps_ref.at[:, :, mine], taps_ref.at[block]),
            (all_decay_ref.at[:, mine], decay_ref.at[block]),
            (all_residue_ref.at[:, mine], residue_ref.at[block]),
            (all_skip_ref.at[:, mine], skip_ref.at[block]),
            (all_tab_ref.at[0, :, lane], tab_ref.at[block, 0]),
        )
        return [
            pltpu.make_async_copy(*pairs[i], load_sem.at[block, i])
            for i in picked
        ]

    load_ids = pltpu.make_async_copy(all_ids_ref, ids_ref, ids_sem.at[0])
    load_ids.start()
    for block in range(2):
        for load in loads(block):
            load.start()
    barrier = pltpu.get_barrier_semaphore()

    def greet(i, _):
        peer = me + i - pieces * ((me + i) // pieces)
        pl.semaphore_signal(barrier, inc=1, device_id={"seq": peer}, device_id_type=MESH)
        return 0

    lax.fori_loop(1, pieces, greet, 0)

    load_ids.wait()
    ids = ids_ref[...]
    before = jnp.where(
        lax.broadcasted_iota(jnp.int32, ids.shape, 0) == 0, -1, pltpu.roll(ids, 1, axis=0)
    )
    entry = lax.broadcasted_iota(jnp.int16, (2 * SUB, vocab), 1)

    count = (HALO + local) // CUTS
    one = jnp.ones(entry.shape, jnp.bfloat16)
    nought = jnp.zeros(entry.shape, jnp.bfloat16)

    def build(slot, i):
        rows = slice(slot * SUB, (slot + 1) * SUB)
        for t in range(i * count - HALO, (i + 1) * count - HALO, 2):
            pair = []
            for at in (t, t + 1):
                column = (
                    ids[rows, at : at + 1] if at >= 0 else before[rows, local + at : local + at + 1]
                )
                pair.append(jnp.broadcast_to(column, (SUB, LANES)))
            pair = jnp.concatenate(pair, axis=0).astype(jnp.int16)
            pair = jnp.concatenate([pair] * (vocab // LANES), axis=1)
            hot_ref[slot, (HALO + t) * SUB : (HALO + t + 2) * SUB, :] = jnp.where(
                pair == entry, one, nought
            )

    everything = pl.ds(0, local)

    def place(block, source, span):
        return out_ref.at[
            span, pl.ds(pl.multiple_of(source * share + block * LANES, LANES), LANES)
        ]

    def remote(block, slot, low, sender, span=everything):
        peer = slot * SUB + low
        return pltpu.make_async_remote_copy(
            src_ref=send_ref.at[block, peer, span],
            dst_ref=place(block, sender, span),
            send_sem=send_sem.at[block, peer],
            recv_sem=recv_sem.at[block, sender],
            device_id={"seq": peer},
            device_id_type=MESH,
        )

    def own(block, span=everything):
        return pltpu.make_async_copy(
            send_ref.at[block, me, span], place(block, me, span), own_sem.at[block]
        )

    cut = (HALO + local) * SUB // CUTS

    def taps_of(block, j):
        return [wide(taps_ref[block, j, lag : lag + 1, :]) for lag in range(width)]

    def mix(rows_ref, taps, i, unroll):
        seen = {}
        for t in range(1 - width, unroll):
            at = pl.multiple_of((i * unroll + t + HALO) * SUB, SUB)
            seen[t] = rows_ref[pl.ds(at, SUB), :]
        totals = []
        for t in range(unroll):
            total = taps[0] * seen[t]
            for lag in range(1, width):
                total = total + taps[lag] * seen[t - lag]
            totals.append(total)
        return totals

    def head(block, slot):
        if block == 0:
            build(slot, 0)
        if slot == 0:
            for load in loads(block, range(6)):
                load.wait()
            rate = decay_ref[block] / length
            coef_ref[0] = jnp.exp(-rate)
            coef_ref[1] = residue_ref[block] * jnp.sqrt(2.0 * rate)
            coef_ref[2] = jnp.exp(-rate * local)
            carry_ref[...] = jnp.zeros_like(carry_ref)

        table = jnp.concatenate([tab_ref[block, j] for j in (1, 2)], axis=1)
        for i in range(CUTS):
            if block == 0 and i + 1 < CUTS:
                build(slot, i + 1)
            span = pl.ds(i * cut, cut)
            x_ref[span, :] = jnp.dot(
                hot_ref[slot, span, :], table, preferred_element_type=jnp.float32
            )
        poles = [wide(coef_ref[0, s : s + 1, :]) for s in range(modes)]
        taps = [taps_of(block, j) for j in (1, 2)]

        def step(i, state):
            state = list(state)
            mixed = [
                mix(x_ref.at[:, j * LANES : (j + 1) * LANES], taps[j], i, LONG) for j in range(2)
            ]
            for t in range(LONG):
                at = pl.multiple_of((i * LONG + t) * SUB, SUB)
                gated = mixed[0][t] * mixed[1][t]
                gated_ref[slot, pl.ds(at, SUB), :] = gated
                for s in range(modes):
                    state[s] = poles[s] * state[s] + gated
            return tuple(state)

        zero = jnp.zeros((SUB, LANES), jnp.float32)
        state = lax.fori_loop(0, local // LONG, step, (zero,) * modes)
        for s in range(modes):
            end_ref[s * SUB : (s + 1) * SUB, :] = state[s]
        leap = coef_ref[2]
        carry = carry_ref[...]
        for k in range(SUB):
            begin_ref[slot, pl.ds(k, modes, stride=SUB), :] = carry
            carry = leap * carry + end_ref[pl.ds(k, modes, stride=SUB), :]
        carry_ref[...] = carry
        if slot == 0:
            for load in loads(block, range(6, 7)):
                load.wait()

    def tail(block, slot, first, heights):
        poles = [wide(coef_ref[0, s : s + 1, :]) for s in range(modes)]
        coefs = [wide(coef_ref[1, s : s + 1, :]) for s in range(modes)]
        skip = wide(skip_ref[block])
        taps = taps_of(block, 0)
        query_ref[...] = jnp.dot(
            hot_ref[slot], tab_ref[block, 0], preferred_element_type=jnp.float32
        )

        def step(i, state):
            state = list(state)
            query = mix(query_ref, taps, i, UNROLL)
            for t in range(UNROLL):
                at = pl.multiple_of((i * UNROLL + t) * SUB, SUB)
                gated = gated_ref[slot, pl.ds(at, SUB), :]
                terms = [skip * gated]
                for s in range(modes):
                    state[s] = poles[s] * state[s] + gated
                    terms.append(coefs[s] * state[s])
                    if len(terms) == 5:
                        terms = [((terms[0] + terms[1]) + (terms[2] + terms[3])) + terms[4]]
                total = terms[0]
                for term in terms[1:]:
                    total = total + term
                turn_ref[pl.ds(at, SUB), :] = query[t] * total
            return tuple(state)

        state = tuple(begin_ref[slot, s * SUB : (s + 1) * SUB, :] for s in range(modes))
        low_end = 0
        for part, height in enumerate(heights):
            start, low_end = low_end, low_end + height
            span = pl.ds(start, height)
            state = lax.fori_loop(start // UNROLL, low_end // UNROLL, step, state)
            for k in range(SUB):
                send_ref[block, slot * SUB + k, span, :] = turn_ref[
                    pl.ds(start * SUB + k, height, stride=SUB), :
                ].astype(jnp.bfloat16)

            if first and part == 0:
                pl.semaphore_wait(barrier, pieces - 1)

            order = FIRST if block == 0 else SECOND
            for k in range(SUB):
                low = k + slot * (order[k] - k)

                @pl.when(slot * SUB + low != me)
                def _():
                    remote(block, slot, low, me, span).start()

            @pl.when(slot == half)
            def _():
                own(block, span).start()

    for block in range(2):
        head(block, 0)
        far = FAR if block == 0 else (local,)

        def early(i, _):
            tail(block, 0, block == 0, far)
            return 0

        lax.fori_loop(0, half, early, 0)
        head(block, 1)

        def far_late(i, _):
            tail(block, 1, block == 0, far)
            return 0

        lax.fori_loop(0, 1 - half, far_late, 0)

        def near_late(i, _):
            tail(block, half, False, (local,))
            return 0

        lax.fori_loop(0, 1, near_late, 0)

    for block in range(2):
        own(block).wait()

        def finish(i, _):
            peer = me + i - pieces * ((me + i) // pieces)
            remote(block, peer // SUB, peer - peer // SUB * SUB, me).wait_send()
            remote(block, half, me - half * SUB, peer).wait_recv()
            return 0

        lax.fori_loop(1, pieces, finish, 0)


def scan_body(token_ids, vocab_table, short_filter, residue, decay, skip_gain):
    pieces = lax.axis_size("seq")
    length = token_ids.shape[0]
    local = length // pieces
    vocab, streams, share = vocab_table.shape
    width = short_filter.shape[0]
    modes = decay.shape[1]
    ids = token_ids.reshape(pieces, local)
    table = vocab_table.transpose(1, 0, 2)
    taps = short_filter.transpose(1, 0, 2)
    rows = (HALO + local) * SUB
    return pl.pallas_call(
        functools.partial(scan_kernel, pieces, local, width, modes),
        out_shape=pltpu.VMEM((local, pieces * share), jnp.bfloat16),
        in_specs=[pl.BlockSpec(memory_space=pl.ANY)] * 6,
        out_specs=pl.BlockSpec(memory_space=pltpu.VMEM),
        scratch_shapes=[
            pltpu.VMEM((pieces, local), jnp.int32),
            pltpu.VMEM((2, streams, vocab, LANES), vocab_table.dtype),
            pltpu.VMEM((2, streams, width, LANES), jnp.float32),
            pltpu.VMEM((2, modes, LANES), jnp.float32),
            pltpu.VMEM((2, modes, LANES), jnp.float32),
            pltpu.VMEM((2, 1, LANES), jnp.float32),
            pltpu.SemaphoreType.DMA((2, 7)),
            pltpu.SemaphoreType.DMA((1,)),
            pltpu.VMEM((2, rows, vocab), jnp.bfloat16),
            pltpu.VMEM((rows, 2 * LANES), jnp.float32),
            pltpu.VMEM((rows, LANES), jnp.float32),
            pltpu.VMEM((2, local * SUB, LANES), jnp.float32),
            pltpu.VMEM((modes * SUB, LANES), jnp.float32),
            pltpu.VMEM((2, modes * SUB, LANES), jnp.float32),
            pltpu.VMEM((modes, LANES), jnp.float32),
            pltpu.VMEM((3, modes, LANES), jnp.float32),
            pltpu.VMEM((local * SUB, LANES), jnp.float32),
            pltpu.VMEM((2, pieces, local, LANES), jnp.bfloat16),
            pltpu.SemaphoreType.DMA((2, pieces)),
            pltpu.SemaphoreType.DMA((2, pieces)),
            pltpu.SemaphoreType.DMA((2,)),
        ],
        compiler_params=pltpu.CompilerParams(collective_id=0, has_side_effects=True),
    )(ids, table, taps, decay.T, residue.T, skip_gain[None])


def fits(mesh, share, local, width, streams):
    even = mesh.shape["seq"] == 2 * SUB
    return even and share == 2 * LANES and local == LANES and width <= HALO + 1 and streams == 3


def solution(mesh):
    placed = (P("groups"), P(None, None, "seq"), P(), P(), P(), P())

    def whole(token_ids, vocab_table, short_filter, residue, decay, skip_gain):
        pieces = mesh.shape["seq"]
        local = token_ids.shape[0] // (mesh.shape["groups"] * pieces)
        share = vocab_table.shape[2] // pieces
        shapes = (share, local, short_filter.shape[0], vocab_table.shape[1])
        chosen = scan_body if fits(mesh, *shapes) else body
        return jax.shard_map(
            chosen, mesh=mesh, in_specs=placed, out_specs=P(("groups", "seq"), None), check_vma=False
        )(token_ids, vocab_table, short_filter, residue, decay, skip_gain)

    return whole
```

```python
import functools
import math

import jax
import jax.numpy as jnp
from jax import lax
from jax.experimental import pallas as pl
from jax.experimental.pallas import tpu as pltpu
from jax.sharding import PartitionSpec as P

HIGHEST = lax.Precision.HIGHEST


def angle_tables(first_index, second_index, modulus):
    product = first_index[:, None] * second_index[None, :] % modulus
    angle = product.astype(jnp.float32) * (2.0 * math.pi / modulus)
    return (jnp.cos(angle), jnp.sin(angle))


def short_conv(padded, taps, count):
    width = taps.shape[0]
    total = jnp.zeros((count,) + padded.shape[1:], jnp.float32)
    for lag in range(width):
        start = width - 1 - lag
        total = total + taps[lag] * padded[start : start + count].astype(jnp.float32)
    return total


def filter_spectrum(freq, total, pole, gap, tail, scale):
    theta = freq.astype(jnp.float32) * (2.0 * math.pi / total)
    sine = jnp.sin(theta)[:, :, None, None]
    halfsq = (jnp.sin(0.5 * theta) ** 2)[:, :, None, None]
    parity = (1 - 2 * (freq % 2)).astype(jnp.float32)[:, :, None, None]
    shape_out = freq.shape + (pole.shape[0],)
    real_part = jnp.zeros(shape_out, jnp.float32)
    imag_part = jnp.zeros(shape_out, jnp.float32)
    for first in range(0, pole.shape[1], 4):
        part_pole = pole[:, first : first + 4]
        dreal = gap[:, first : first + 4] + 2.0 * part_pole * halfsq
        dimag = part_pole * sine
        factor = (
            scale[:, first : first + 4]
            * (1.0 - tail[:, first : first + 4] * parity)
            / (dreal * dreal + dimag * dimag)
        )
        real_part = real_part + jnp.sum(factor * dreal, axis=-1)
        imag_part = imag_part - jnp.sum(factor * dimag, axis=-1)
    return (real_part, imag_part)


def convolve(gated, skip, filters, total, move_forward, move_back):
    pieces, block, width = gated.shape
    span = 2 * pieces
    outer_index = jnp.arange(span, dtype=jnp.int32)
    piece_index = jnp.arange(pieces, dtype=jnp.int32)
    outer_cos, outer_sin = angle_tables(outer_index, piece_index, span)
    real_part = jnp.einsum("kp,ptc->ktc", outer_cos, gated, precision=HIGHEST)
    imag_part = -jnp.einsum("kp,ptc->ktc", outer_sin, gated, precision=HIGHEST)
    times = jnp.arange(block, dtype=jnp.int32)
    twist_cos, twist_sin = angle_tables(outer_index, times, total)
    twist_cos = twist_cos[:, :, None]
    twist_sin = twist_sin[:, :, None]
    turned_real = twist_cos * real_part + twist_sin * imag_part
    turned_imag = twist_cos * imag_part - twist_sin * real_part
    moved = move_forward(jnp.stack([turned_real, turned_imag]))
    count = moved.shape[1]
    length = moved.shape[2]
    positions = jnp.arange(length, dtype=jnp.int32)
    inner_cos, inner_sin = angle_tables(positions, positions, length)
    freq_real = jnp.einsum("mt,ktc->kmc", inner_cos, moved[0], precision=HIGHEST) + jnp.einsum(
        "mt,ktc->kmc", inner_sin, moved[1], precision=HIGHEST
    )
    freq_imag = jnp.einsum("mt,ktc->kmc", inner_cos, moved[1], precision=HIGHEST) - jnp.einsum(
        "mt,ktc->kmc", inner_sin, moved[0], precision=HIGHEST
    )
    owned = jnp.arange(count, dtype=jnp.int32)
    freq = (owned[:, None] + span * positions[None, :]) % total
    filt_real, filt_imag = filter_spectrum(freq, total, *filters)
    prod_real = freq_real * filt_real - freq_imag * filt_imag
    prod_imag = freq_real * filt_imag + freq_imag * filt_real
    back_real = jnp.einsum("mt,kmc->ktc", inner_cos, prod_real, precision=HIGHEST) - jnp.einsum(
        "mt,kmc->ktc", inner_sin, prod_imag, precision=HIGHEST
    )
    back_imag = jnp.einsum("mt,kmc->ktc", inner_cos, prod_imag, precision=HIGHEST) + jnp.einsum(
        "mt,kmc->ktc", inner_sin, prod_real, precision=HIGHEST
    )
    undo_cos, undo_sin = angle_tables(owned, positions, total)
    undo_cos = undo_cos[:, :, None]
    undo_sin = undo_sin[:, :, None]
    untwist_real = undo_cos * back_real - undo_sin * back_imag
    untwist_imag = undo_cos * back_imag + undo_sin * back_real
    returned = move_back(jnp.stack([untwist_real, untwist_imag]))
    last_cos, last_sin = angle_tables(piece_index, outer_index, span)
    convolved = (
        jnp.einsum("pk,ktc->ptc", last_cos, returned[0], precision=HIGHEST)
        - jnp.einsum("pk,ktc->ptc", last_sin, returned[1], precision=HIGHEST)
    ) * (1.0 / total)
    return convolved + skip * gated


def unchanged(value):
    return value


def body(token_ids, vocab_table, short_filter, residue, decay, skip_gain):
    pieces = lax.axis_size("seq")
    place = lax.axis_index("seq")
    length = token_ids.shape[0]
    local = length // pieces
    share = vocab_table.shape[2]
    rim = short_filter.shape[0] - 1
    total = 2 * length
    rate = decay / length
    pole = jnp.exp(-rate)
    gap = -jnp.expm1(-rate)
    tail = jnp.exp(-decay)
    scale = residue * jnp.sqrt(2.0 * rate)
    first_channel = place * share
    chan_taps = lax.dynamic_slice_in_dim(short_filter, first_channel, share, 2)
    chan_filters = (
        lax.dynamic_slice_in_dim(pole, first_channel, share, 0),
        lax.dynamic_slice_in_dim(gap, first_channel, share, 0),
        lax.dynamic_slice_in_dim(tail, first_channel, share, 0),
        lax.dynamic_slice_in_dim(scale, first_channel, share, 0),
    )
    chan_skip = lax.dynamic_slice_in_dim(skip_gain, first_channel, share, 0)
    entries = jnp.arange(vocab_table.shape[0], dtype=token_ids.dtype)
    chosen = (token_ids[:, None] == entries[None, :]).astype(vocab_table.dtype)
    streams = jnp.einsum("nv,vjc->njc", chosen, vocab_table, preferred_element_type=jnp.float32)
    padded = jnp.pad(streams, ((rim, 0), (0, 0), (0, 0)))
    mixed = short_conv(padded, chan_taps, length)
    query = mixed[:, 0]
    gated = (mixed[:, 1] * mixed[:, 2]).reshape(pieces, local, share)
    convolved = convolve(gated, chan_skip, chan_filters, total, unchanged, unchanged)
    output = (query * convolved.reshape(length, share)).astype(jnp.bfloat16)
    return lax.all_to_all(output, "seq", split_axis=0, concat_axis=1, tiled=True)


LANES = 128
SUB = 8
HALO = 8
LONG = 32
FIRST = (0, 1, 2, 3, 4, 5, 6, 7)
SECOND = (0, 4, 1, 5, 2, 6, 3, 7)
UNROLL = 16
CUTS = 4
FAR = (16, 32, 80,)
MESH = pl.DeviceIdType.MESH


def wide(row):
    return jnp.broadcast_to(row, (SUB, LANES))


def scan_kernel(
    pieces,
    local,
    width,
    modes,
    all_ids_ref,
    all_tab_ref,
    all_taps_ref,
    all_decay_ref,
    all_residue_ref,
    all_skip_ref,
    out_ref,
    ids_ref,
    tab_ref,
    taps_ref,
    decay_ref,
    residue_ref,
    skip_ref,
    load_sem,
    ids_sem,
    hot_ref,
    x_ref,
    query_ref,
    gated_ref,
    end_ref,
    begin_ref,
    carry_ref,
    coef_ref,
    turn_ref,
    send_ref,
    send_sem,
    recv_sem,
    own_sem,
):
    me = lax.axis_index("seq")
    half = me // SUB
    share = 2 * LANES
    vocab = tab_ref.shape[2]
    length = pieces * local

    def loads(block, picked=range(7)):
        mine = pl.ds(pl.multiple_of(me * share + block * LANES, LANES), LANES)
        lane = pl.ds(block * LANES, LANES)
        pairs = (
            (all_tab_ref.at[1, :, lane], tab_ref.at[block, 1]),
            (all_tab_ref.at[2, :, lane], tab_ref.at[block, 2]),
            (all_taps_ref.at[:, :, mine], taps_ref.at[block]),
            (all_decay_ref.at[:, mine], decay_ref.at[block]),
            (all_residue_ref.at[:, mine], residue_ref.at[block]),
            (all_skip_ref.at[:, mine], skip_ref.at[block]),
            (all_tab_ref.at[0, :, lane], tab_ref.at[block, 0]),
        )
        return [
            pltpu.make_async_copy(*pairs[i], load_sem.at[block, i])
            for i in picked
        ]

    load_ids = pltpu.make_async_copy(all_ids_ref, ids_ref, ids_sem.at[0])
    load_ids.start()
    for block in range(2):
        for load in loads(block):
            load.start()
    barrier = pltpu.get_barrier_semaphore()

    def greet(i, _):
        peer = me + i - pieces * ((me + i) // pieces)
        pl.semaphore_signal(barrier, inc=1, device_id={"seq": peer}, device_id_type=MESH)
        return 0

    lax.fori_loop(1, pieces, greet, 0)

    load_ids.wait()
    ids = ids_ref[...]
    before = jnp.where(
        lax.broadcasted_iota(jnp.int32, ids.shape, 0) == 0, -1, pltpu.roll(ids, 1, axis=0)
    )
    entry = lax.broadcasted_iota(jnp.int16, (2 * SUB, vocab), 1)

    count = (HALO + local) // CUTS
    one = jnp.ones(entry.shape, jnp.bfloat16)
    nought = jnp.zeros(entry.shape, jnp.bfloat16)

    def build(slot, i):
        rows = slice(slot * SUB, (slot + 1) * SUB)
        for t in range(i * count - HALO, (i + 1) * count - HALO, 2):
            pair = []
            for at in (t, t + 1):
                column = (
                    ids[rows, at : at + 1] if at >= 0 else before[rows, local + at : local + at + 1]
                )
                pair.append(jnp.broadcast_to(column, (SUB, LANES)))
            pair = jnp.concatenate(pair, axis=0).astype(jnp.int16)
            pair = jnp.concatenate([pair] * (vocab // LANES), axis=1)
            hot_ref[slot, (HALO + t) * SUB : (HALO + t + 2) * SUB, :] = jnp.where(
                pair == entry, one, nought
            )

    everything = pl.ds(0, local)

    def place(block, source, span):
        return out_ref.at[
            span, pl.ds(pl.multiple_of(source * share + block * LANES, LANES), LANES)
        ]

    def remote(block, slot, low, sender, span=everything):
        peer = slot * SUB + low
        return pltpu.make_async_remote_copy(
            src_ref=send_ref.at[block, peer, span],
            dst_ref=place(block, sender, span),
            send_sem=send_sem.at[block, peer],
            recv_sem=recv_sem.at[block, sender],
            device_id={"seq": peer},
            device_id_type=MESH,
        )

    def own(block, span=everything):
        return pltpu.make_async_copy(
            send_ref.at[block, me, span], place(block, me, span), own_sem.at[block]
        )

    cut = (HALO + local) * SUB // CUTS

    def taps_of(block, j):
        return [wide(taps_ref[block, j, lag : lag + 1, :]) for lag in range(width)]

    def mix(rows_ref, taps, i, unroll):
        seen = {}
        for t in range(1 - width, unroll):
            at = pl.multiple_of((i * unroll + t + HALO) * SUB, SUB)
            seen[t] = rows_ref[pl.ds(at, SUB), :]
        totals = []
        for t in range(unroll):
            total = taps[0] * seen[t]
            for lag in range(1, width):
                total = total + taps[lag] * seen[t - lag]
            totals.append(total)
        return totals

    def head(block, slot):
        if block == 0:
            if slot == 0:
                build(0, 0)
                build(1, 0)
                build(1, 1)
        if slot == 0:
            for load in loads(block, range(6)):
                load.wait()
            rate = decay_ref[block] / length
            coef_ref[0] = jnp.exp(-rate)
            coef_ref[1] = residue_ref[block] * jnp.sqrt(2.0 * rate)
            coef_ref[2] = jnp.exp(-rate * local)
            carry_ref[...] = jnp.zeros_like(carry_ref)

        table = jnp.concatenate([tab_ref[block, j] for j in (1, 2)], axis=1)
        for i in range(CUTS):
            if block == 0 and i + 1 < CUTS and (slot, i) != (1, 0):
                build(slot, i + 1)
            span = pl.ds(i * cut, cut)
            x_ref[span, :] = jnp.dot(
                hot_ref[slot, span, :], table, preferred_element_type=jnp.float32
            )
        poles = [wide(coef_ref[0, s : s + 1, :]) for s in range(modes)]
        taps = [taps_of(block, j) for j in (1, 2)]

        def step(i, state):
            state = list(state)
            mixed = [
                mix(x_ref.at[:, j * LANES : (j + 1) * LANES], taps[j], i, LONG) for j in range(2)
            ]
            for t in range(LONG):
                at = pl.multiple_of((i * LONG + t) * SUB, SUB)
                gated = mixed[0][t] * mixed[1][t]
                gated_ref[slot, pl.ds(at, SUB), :] = gated
                for s in range(modes):
                    state[s] = poles[s] * state[s] + gated
            return tuple(state)

        zero = jnp.zeros((SUB, LANES), jnp.float32)
        state = lax.fori_loop(0, local // LONG, step, (zero,) * modes)
        for s in range(modes):
            end_ref[s * SUB : (s + 1) * SUB, :] = state[s]
        leap = coef_ref[2]
        carry = carry_ref[...]
        for k in range(SUB):
            begin_ref[slot, pl.ds(k, modes, stride=SUB), :] = carry
            carry = leap * carry + end_ref[pl.ds(k, modes, stride=SUB), :]
        carry_ref[...] = carry
        if slot == 0:
            for load in loads(block, range(6, 7)):
                load.wait()

    def tail(block, slot, first, heights):
        poles = [wide(coef_ref[0, s : s + 1, :]) for s in range(modes)]
        coefs = [wide(coef_ref[1, s : s + 1, :]) for s in range(modes)]
        skip = wide(skip_ref[block])
        taps = taps_of(block, 0)
        query_ref[...] = jnp.dot(
            hot_ref[slot], tab_ref[block, 0], preferred_element_type=jnp.float32
        )

        def step(i, state):
            state = list(state)
            query = mix(query_ref, taps, i, UNROLL)
            for t in range(UNROLL):
                at = pl.multiple_of((i * UNROLL + t) * SUB, SUB)
                gated = gated_ref[slot, pl.ds(at, SUB), :]
                terms = [skip * gated]
                for s in range(modes):
                    state[s] = poles[s] * state[s] + gated
                    terms.append(coefs[s] * state[s])
                    if len(terms) == 5:
                        terms = [((terms[0] + terms[1]) + (terms[2] + terms[3])) + terms[4]]
                total = terms[0]
                for term in terms[1:]:
                    total = total + term
                turn_ref[pl.ds(at, SUB), :] = query[t] * total
            return tuple(state)

        state = tuple(begin_ref[slot, s * SUB : (s + 1) * SUB, :] for s in range(modes))
        low_end = 0
        for part, height in enumerate(heights):
            start, low_end = low_end, low_end + height
            span = pl.ds(start, height)
            state = lax.fori_loop(start // UNROLL, low_end // UNROLL, step, state)
            for k in range(SUB):
                send_ref[block, slot * SUB + k, span, :] = turn_ref[
                    pl.ds(start * SUB + k, height, stride=SUB), :
                ].astype(jnp.bfloat16)

            if first and part == 0:
                pl.semaphore_wait(barrier, pieces - 1)

            order = FIRST if block == 0 else SECOND
            for k in range(SUB):
                low = k + slot * (order[k] - k)

                @pl.when(slot * SUB + low != me)
                def _():
                    remote(block, slot, low, me, span).start()

            @pl.when(slot == half)
            def _():
                own(block, span).start()

    for block in range(2):
        head(block, 0)
        far = FAR if block == 0 else (local,)

        def early(i, _):
            tail(block, 0, block == 0, far)
            return 0

        lax.fori_loop(0, half, early, 0)
        head(block, 1)

        def far_late(i, _):
            tail(block, 1, block == 0, far)
            return 0

        lax.fori_loop(0, 1 - half, far_late, 0)

        def near_late(i, _):
            tail(block, half, False, (local,))
            return 0

        lax.fori_loop(0, 1, near_late, 0)

    for block in range(2):
        own(block).wait()

        def finish(i, _):
            peer = me + i - pieces * ((me + i) // pieces)
            remote(block, peer // SUB, peer - peer // SUB * SUB, me).wait_send()
            remote(block, half, me - half * SUB, peer).wait_recv()
            return 0

        lax.fori_loop(1, pieces, finish, 0)


def scan_body(token_ids, vocab_table, short_filter, residue, decay, skip_gain):
    pieces = lax.axis_size("seq")
    length = token_ids.shape[0]
    local = length // pieces
    vocab, streams, share = vocab_table.shape
    width = short_filter.shape[0]
    modes = decay.shape[1]
    ids = token_ids.reshape(pieces, local)
    table = vocab_table.transpose(1, 0, 2)
    taps = short_filter.transpose(1, 0, 2)
    rows = (HALO + local) * SUB
    return pl.pallas_call(
        functools.partial(scan_kernel, pieces, local, width, modes),
        out_shape=pltpu.VMEM((local, pieces * share), jnp.bfloat16),
        in_specs=[pl.BlockSpec(memory_space=pl.ANY)] * 6,
        out_specs=pl.BlockSpec(memory_space=pltpu.VMEM),
        scratch_shapes=[
            pltpu.VMEM((pieces, local), jnp.int32),
            pltpu.VMEM((2, streams, vocab, LANES), vocab_table.dtype),
            pltpu.VMEM((2, streams, width, LANES), jnp.float32),
            pltpu.VMEM((2, modes, LANES), jnp.float32),
            pltpu.VMEM((2, modes, LANES), jnp.float32),
            pltpu.VMEM((2, 1, LANES), jnp.float32),
            pltpu.SemaphoreType.DMA((2, 7)),
            pltpu.SemaphoreType.DMA((1,)),
            pltpu.VMEM((2, rows, vocab), jnp.bfloat16),
            pltpu.VMEM((rows, 2 * LANES), jnp.float32),
            pltpu.VMEM((rows, LANES), jnp.float32),
            pltpu.VMEM((2, local * SUB, LANES), jnp.float32),
            pltpu.VMEM((modes * SUB, LANES), jnp.float32),
            pltpu.VMEM((2, modes * SUB, LANES), jnp.float32),
            pltpu.VMEM((modes, LANES), jnp.float32),
            pltpu.VMEM((3, modes, LANES), jnp.float32),
            pltpu.VMEM((local * SUB, LANES), jnp.float32),
            pltpu.VMEM((2, pieces, local, LANES), jnp.bfloat16),
            pltpu.SemaphoreType.DMA((2, pieces)),
            pltpu.SemaphoreType.DMA((2, pieces)),
            pltpu.SemaphoreType.DMA((2,)),
        ],
        compiler_params=pltpu.CompilerParams(collective_id=0, has_side_effects=True),
    )(ids, table, taps, decay.T, residue.T, skip_gain[None])


def fits(mesh, share, local, width, streams):
    even = mesh.shape["seq"] == 2 * SUB
    return even and share == 2 * LANES and local == LANES and width <= HALO + 1 and streams == 3


def solution(mesh):
    placed = (P("groups"), P(None, None, "seq"), P(), P(), P(), P())

    def whole(token_ids, vocab_table, short_filter, residue, decay, skip_gain):
        pieces = mesh.shape["seq"]
        local = token_ids.shape[0] // (mesh.shape["groups"] * pieces)
        share = vocab_table.shape[2] // pieces
        shapes = (share, local, short_filter.shape[0], vocab_table.shape[1])
        chosen = scan_body if fits(mesh, *shapes) else body
        return jax.shard_map(
            chosen, mesh=mesh, in_specs=placed, out_specs=P(("groups", "seq"), None), check_vma=False
        )(token_ids, vocab_table, short_filter, residue, decay, skip_gain)

    return whole
```
